32 devices in a mesh: rev: 8 (over y, x, core), row: 4 (over z).
Axes of the slice: x: 2, y: 2, z: 4, core: 2. Of those that a mesh axis runs over, the one named last changes fastest.
Arguments:
- fields: bfloat16 [8, 16, 1024, 1024], P('rev', None, 'row'), may hold values from -6 to 6
- out_grads: bfloat16 [8, 16, 1024, 1024], P('rev', None, 'row'), may hold values from -6 to 6
- partner: int32 [8], replicated, may hold values from 0 to 7, as said below
- kept_blocks: int32 [8], replicated, may hold values from 1 to 8
- weight_in: float32 [1, 2, 32, 16], replicated, may hold values from -0.75 to 0.75
- bias_in: float32 [1, 2, 16], replicated, may hold values from -3 to 3
- weight_out: float32 [1, 2, 16, 16], replicated, may hold values from -1 to 1
Outputs:
- field_grads: bfloat16 [8, 16, 1024, 1024], P('rev', None, 'row')
- grad_weight_in: float32 [1, 2, 32, 16], replicated
- grad_bias_in: float32 [1, 2, 16], replicated
- grad_weight_out: float32 [1, 2, 16, 16], replicated
- grad_bias_out: float32 [1, 2, 16], replicated
The draws below stay inside these ranges and needn't reach their ends.
Inputs may be any that keep to these rules, and one draw needn't show every extreme that they name: partner[partner[r]] = r and partner[r] != r for every revision r; some revision r has partner[r] = (r + 4) mod 8.
All inputs are finite; a program needn't handle non-finite values.
Results may differ from the reference program's by a relative error of at most 0.01.
Values may be sent and summed in bfloat16 or wider, within the bound.
A program may use at most 128 MiB of HBM per device.

```python
import math
import jax
import jax.numpy as jnp
from jax import lax

NH = 1024
NW = 1024
BS = 16
BLOCKS = 1
KX = 128
MB = 16
KY = 256
C = 16
REVS = 8


def draw_partner(key, part):
    first = jax.random.randint(jax.random.fold_in(key, 3), (), 0, REVS).astype(jnp.int32)
    second = ((first + REVS // 2) % REVS).astype(jnp.int32)
    scores = jax.random.permutation(key, REVS).astype(jnp.int32)
    scores = scores.at[first].set(-2)
    scores = scores.at[second].set(-1)
    order = jnp.argsort(scores, stable=True).astype(jnp.int32)
    swapped = order.reshape(REVS // 2, 2)[:, ::-1].reshape(REVS)
    return jnp.zeros((REVS,), jnp.int32).at[order].set(swapped)


def draw_kept_blocks(key, part):
    most = KX // MB
    values = jax.random.randint(key, (REVS,), 1, most + 1).astype(jnp.int32)
    places = jax.random.permutation(jax.random.fold_in(key, 7), REVS).astype(jnp.int32)
    values = values.at[places[0]].set(most)
    values = values.at[places[1]].set(1)
    return values


def block_levels(stream_key, shape, split, least, largest):
    loudness = 1.0
    for position, parts in split:
        draws = jax.random.uniform(jax.random.fold_in(jax.random.fold_in(stream_key, 6), position), (parts,), jnp.float32, least / len(split), largest / len(split))
        loudness = loudness * jnp.repeat(jnp.exp(draws), shape[position] // parts).reshape((-1,) + (1,) * (len(shape) - 1 - position))
    return loudness


def normal_values(key, shape, width, most, shards=(), held_as=jnp.bfloat16):
    result = width * jax.random.normal(key, shape, jnp.float32)
    if shards:
        result = result * block_levels(key, shape, shards, -0.22, 0.18)
    return jnp.clip(result, -most, most).astype(held_as)


def setup_inputs(seed: int = 0) -> dict:
    splits = jax.random.split(jax.random.key(seed), 8)
    return {
        "fields": normal_values(splits[0], (REVS, C, NH, NW), 1.0, 6.0, ((0, 8), (2, 4))),
        "out_grads": normal_values(splits[1], (REVS, C, NH, NW), 1.0, 6.0, ((0, 8), (2, 4))),
        "partner": draw_partner(jax.random.fold_in(splits[7], 71), 0),
        "kept_blocks": draw_kept_blocks(jax.random.fold_in(splits[7], 71), 0),
        "weight_in": normal_values(splits[4], (BLOCKS, 2, 2 * BS, BS), (4 * BS) ** -0.5, 0.75, (), jnp.float32),
        "bias_in": normal_values(splits[5], (BLOCKS, 2, BS), 0.5, 3.0, (), jnp.float32),
        "weight_out": normal_values(splits[6], (BLOCKS, 2, BS, BS), (2 * BS) ** -0.5, 1.0, (), jnp.float32),
    }


HIGHEST = lax.Precision.HIGHEST

def column_tables(n_cols, n_keep):
    col_index = jnp.arange(n_cols, dtype=jnp.int32)[:, None]
    freq_index = jnp.arange(n_keep, dtype=jnp.int32)[None, :]
    phases = col_index * freq_index % n_cols
    angles = phases.astype(jnp.float32) * (2.0 * math.pi / n_cols)
    return (jnp.cos(angles).astype(jnp.bfloat16), jnp.sin(angles).astype(jnp.bfloat16))

def row_tables(n_rows, n_keep):
    row_index = jnp.arange(n_rows, dtype=jnp.int32)[None, :]
    slot_index = jnp.arange(n_keep, dtype=jnp.int32)
    signed = jnp.where(slot_index < n_keep // 2, slot_index, slot_index - n_keep + n_rows)
    phases = signed[:, None] * row_index % n_rows
    angles = phases.astype(jnp.float32) * (2.0 * math.pi / n_rows)
    return (jnp.cos(angles).astype(jnp.bfloat16), jnp.sin(angles).astype(jnp.bfloat16))

def keep_mask(kept_count, col_index, n_keep):
    slot_index = jnp.arange(n_keep, dtype=jnp.int32)
    row_extent = jnp.where(slot_index < n_keep // 2, slot_index, n_keep - slot_index)
    extent = jnp.maximum(col_index[:, None], row_extent[None, :])
    return (extent < kept_count * MB).astype(jnp.float32)

def complex_layer(weights, biases, real_part, imag_part):

    def mixing(matrix, values):
        return jnp.einsum('bio,bipq->bopq', matrix, values, precision=HIGHEST)
    weight_real = weights[:, 0]
    weight_imag = weights[:, 1]
    out_real = mixing(weight_real, real_part) - mixing(weight_imag, imag_part) + biases[:, 0, :, None, None]
    out_imag = mixing(weight_imag, real_part) + mixing(weight_real, imag_part) + biases[:, 1, :, None, None]
    return (out_real, out_imag)

def spectral_mlp(params, own_spec, other_spec):
    weight_in, bias_in, weight_out, bias_out = params
    blocks = weight_in.shape[0]
    block_width = own_spec.shape[1] // blocks
    trailing = own_spec.shape[2:]

    def split_blocks(spectrum):
        return spectrum.reshape((2, blocks, block_width) + trailing)
    joined = jnp.concatenate([split_blocks(own_spec), split_blocks(other_spec)], axis=2)
    hidden_real, hidden_imag = complex_layer(weight_in, bias_in, joined[0], joined[1])
    hidden_real = jax.nn.gelu(hidden_real, approximate=True)
    hidden_imag = jax.nn.gelu(hidden_imag, approximate=True)
    out_real, out_imag = complex_layer(weight_out, bias_out, hidden_real, hidden_imag)
    return jnp.stack([out_real, out_imag]).reshape((2, blocks * block_width) + trailing)

def mlp_backward(params, own_spec, other_spec, cotangent):
    unused, pullback = jax.vjp(spectral_mlp, params, own_spec, other_spec)
    return pullback(cotangent)

def row_spectrum(column_spec, row_cos, row_sin):
    data = column_spec.astype(jnp.float32)
    with_cos = jnp.einsum('schk,jh->sckj', data, row_cos.astype(jnp.float32))
    with_sin = jnp.einsum('schk,jh->sckj', data, row_sin.astype(jnp.float32))
    real_part = with_cos[0] + with_sin[1]
    imag_part = with_cos[1] - with_sin[0]
    return jnp.stack([real_part, imag_part]) * (1.0 / math.sqrt(NH * NW))

def forward_spectrum(field, col_cos, col_sin, row_cos, row_sin):
    channels, n_rows, n_cols = field.shape
    flattened = field.reshape(channels * n_rows, n_cols)
    real_cols = jnp.dot(flattened, col_cos, preferred_element_type=jnp.float32)
    imag_cols = -jnp.dot(flattened, col_sin, preferred_element_type=jnp.float32)
    column_spec = jnp.stack([real_cols, imag_cols]).astype(jnp.bfloat16).reshape(2, channels, n_rows, -1)
    return row_spectrum(column_spec, row_cos, row_sin)

def inverse_rows(total, row_cos, row_sin):
    data = total.astype(jnp.float32)
    with_cos = jnp.einsum('sckj,jh->schk', data, row_cos.astype(jnp.float32))
    with_sin = jnp.einsum('sckj,jh->schk', data, row_sin.astype(jnp.float32))
    real_part = with_cos[0] - with_sin[1]
    imag_part = with_sin[0] + with_cos[1]
    return jnp.stack([real_part, imag_part]).astype(jnp.bfloat16)

def inverse_cols(rows_spec, col_cos, col_sin):
    channels, n_rows, n_keep = rows_spec.shape[1:]
    real_rows = rows_spec[0].reshape(channels * n_rows, n_keep)
    imag_rows = rows_spec[1].reshape(channels * n_rows, n_keep)
    result_real = jnp.einsum('hk,wk->hw', real_rows.astype(jnp.float32), col_cos.astype(jnp.float32))
    result_imag = jnp.einsum('hk,wk->hw', imag_rows.astype(jnp.float32), col_sin.astype(jnp.float32))
    field = (result_real - result_imag) * (1.0 / math.sqrt(NH * NW))
    return field.astype(jnp.bfloat16).reshape(channels, n_rows, -1)

def reference(fields, out_grads, partner, kept_blocks, weight_in, bias_in, weight_out):
    col_cos, col_sin = column_tables(NW, KX)
    row_cos, row_sin = row_tables(NH, KY)

    def spectrum_of(field):
        return forward_spectrum(field, col_cos, col_sin, row_cos, row_sin)
    spectra = lax.map(spectrum_of, fields)
    grad_spec = lax.map(spectrum_of, out_grads)
    shared = spectra.astype(jnp.bfloat16)
    partner_spec = jnp.take(shared, partner, axis=0).astype(jnp.float32)
    col_index = jnp.arange(KX, dtype=jnp.int32)
    masks = jax.vmap(lambda kept: keep_mask(kept, col_index, KY))(kept_blocks)
    params = (weight_in, bias_in, weight_out, jnp.zeros_like(bias_in))

    def per_revision(inputs):
        own_spec, other_spec, grad_part, mask_part = inputs
        return mlp_backward(params, own_spec, other_spec, grad_part * mask_part[None, None])
    param_grads, own_grads, other_grads = lax.map(per_revision, (spectra, partner_spec, grad_spec, masks))
    returned = other_grads.astype(jnp.bfloat16)
    total = (own_grads + jnp.take(returned, partner, axis=0).astype(jnp.float32)).astype(jnp.bfloat16)

    def inverse_of(revision):
        return inverse_cols(inverse_rows(revision, row_cos, row_sin), col_cos, col_sin)
    field_grads = lax.map(inverse_of, total)
    grad_scale = 1.0 / math.sqrt(REVS * KX * KY)
    summed = [lax.optimization_barrier(jnp.sum(stacked, axis=0)) * grad_scale for stacked in param_grads]
    return (field_grads, summed[0], summed[1], summed[2], summed[3])
```

```python
import functools
import math

import jax
import jax.numpy as jnp
import ml_dtypes
import numpy as np
from jax import lax
from jax.experimental import pallas as pl
from jax.experimental.pallas import tpu as pltpu
from jax.sharding import PartitionSpec as P

KX = 128
MB = 16
KY = 256
BF16 = jnp.bfloat16
F32 = jnp.float32
GELU_A = math.sqrt(2.0 / math.pi)
GELU_B = 0.044715


def column_tables(n_cols):
    phases = np.arange(n_cols)[:, None] * np.arange(KX)[None, :] % n_cols
    angles = phases.astype(np.float32) * np.float32(2.0 * math.pi / n_cols)
    both = np.concatenate([np.cos(angles), -np.sin(angles)], axis=1)
    return both.astype(ml_dtypes.bfloat16)


def row_tables(n_rows, shards):
    slot = np.arange(KY)
    signed = np.where(slot < KY // 2, slot, slot - KY + n_rows)
    phases = signed[:, None] * np.arange(n_rows)[None, :] % n_rows
    angles = phases.astype(np.float32) * np.float32(2.0 * math.pi / n_rows)
    both = np.concatenate([np.cos(angles), np.sin(angles)], axis=0)
    split = both.reshape(2 * KY, shards, n_rows // shards).transpose(1, 0, 2)
    return np.ascontiguousarray(split).astype(ml_dtypes.bfloat16)


def forward_kernel(channels, scale, x_ref, col_ref, row_ref, out_ref, held):
    step = pl.program_id(0)
    cols = jnp.dot(x_ref[0], col_ref[...], preferred_element_type=F32).astype(BF16)
    quads = jnp.dot(row_ref[...], cols, preferred_element_type=F32)
    real = (quads[:KY, :KX] + quads[KY:, KX:]) * scale
    imag = (quads[:KY, KX:] - quads[KY:, :KX]) * scale
    held[pl.ds(pl.multiple_of(step * KY, KY), KY), :] = real
    held[pl.ds(pl.multiple_of((channels + step) * KY, KY), KY), :] = imag

    @pl.when(step == channels - 1)
    def _():
        def turn(j, carry):
            out_ref[j] = held[pl.ds(j, 2 * channels, stride=KY), :].astype(BF16)
            return carry

        lax.fori_loop(0, KY, turn, 0, unroll=8)


def forward_partial(field, col_table, row_table, scale):
    channels, n_rows, n_cols = field.shape
    return pl.pallas_call(
        functools.partial(forward_kernel, channels, scale),
        grid=(channels,),
        out_shape=jax.ShapeDtypeStruct((KY, 2 * channels, KX), BF16),
        in_specs=[
            pl.BlockSpec((1, n_rows, n_cols), lambda c: (c, 0, 0)),
            pl.BlockSpec((n_cols, 2 * KX), lambda c: (0, 0)),
            pl.BlockSpec((2 * KY, n_rows), lambda c: (0, 0)),
        ],
        out_specs=pl.BlockSpec((KY, 2 * channels, KX), lambda c: (0, 0, 0)),
        scratch_shapes=[pltpu.VMEM((2 * channels * KY, KX), F32)],
        compiler_params=pltpu.CompilerParams(
            dimension_semantics=("arbitrary",), vmem_limit_bytes=32 << 20
        ),
        cost_estimate=pl.CostEstimate(
            flops=channels * n_rows * 2 * KX * (2 * n_cols + 4 * KY),
            bytes_accessed=2 * field.size + 4 * KY * channels * KX,
            transcendentals=0,
        ),
    )(field, col_table, row_table)


def inverse_kernel(channels, scale, total_ref, row_ref, col_ref, out_ref, held):
    step = pl.program_id(0)

    @pl.when(step == 0)
    def _():
        def turn(j, carry):
            at = pl.multiple_of(j * 2 * channels, 2 * channels)
            held[pl.ds(at, 2 * channels), :] = total_ref[j].astype(F32)
            return carry

        lax.fori_loop(0, KY, turn, 0, unroll=8)

    real = held[pl.ds(step, KY, stride=2 * channels), :].astype(BF16)
    imag = held[pl.ds(channels + step, KY, stride=2 * channels), :].astype(BF16)
    pair = jnp.concatenate([real, imag], axis=1)
    n_rows = out_ref.shape[1]
    quads = lax.dot_general(
        row_ref[...], pair, (((1,), (0,)), ((), ())), preferred_element_type=F32
    )
    rows_re = quads[:n_rows, :KX] - quads[n_rows:, KX:]
    rows_im = quads[n_rows:, :KX] + quads[:n_rows, KX:]
    rows = jnp.concatenate([rows_re, rows_im], axis=1).astype(BF16)
    field = jnp.dot(rows, col_ref[...], preferred_element_type=F32) * scale
    out_ref[0] = field.astype(BF16)


def inverse_field(total, row_table_t, col_table_t, scale):
    channels = total.shape[1] // 2
    n_rows, n_cols = row_table_t.shape[0] // 2, col_table_t.shape[1]
    return pl.pallas_call(
        functools.partial(inverse_kernel, channels, scale),
        grid=(channels,),
        out_shape=jax.ShapeDtypeStruct((channels, n_rows, n_cols), BF16),
        in_specs=[
            pl.BlockSpec((KY, 2 * channels, KX), lambda c: (0, 0, 0)),
            pl.BlockSpec((2 * n_rows, KY), lambda c: (0, 0)),
            pl.BlockSpec((2 * KX, n_cols), lambda c: (0, 0)),
        ],
        out_specs=pl.BlockSpec((1, n_rows, n_cols), lambda c: (c, 0, 0)),
        scratch_shapes=[pltpu.VMEM((2 * channels * KY, KX), F32)],
        compiler_params=pltpu.CompilerParams(
            dimension_semantics=("arbitrary",), vmem_limit_bytes=32 << 20
        ),
        cost_estimate=pl.CostEstimate(
            flops=channels * n_rows * 2 * KX * (2 * n_cols + 4 * KY),
            bytes_accessed=2 * channels * n_rows * n_cols + 4 * KY * channels * KX,
            transcendentals=0,
        ),
    )(total, row_table_t, col_table_t)


def mlp_kernel(
    slots, group, width, slot0_ref, kept_ref, own_ref, other_ref, cot_ref, win_ref, bias_ref,
    wout_t_ref, win_t_ref, own_out, other_out, sums_ref,
):
    step = pl.program_id(0)

    @pl.when(step == 0)
    def _():
        sums_ref[...] = jnp.zeros_like(sums_ref)

    lanes = lax.broadcasted_iota(jnp.int32, (width, KX), 1)
    limit = kept_ref[0] * MB
    own, other, cot = [], [], []
    for g in range(group):
        slot = slot0_ref[0] + step * group + g
        extent = jnp.where(slot < KY // 2, slot, KY - slot)
        keep = jnp.maximum(lanes, extent) < limit
        own.append(own_ref[g])
        other.append(other_ref[g])
        cot.append(jnp.where(keep, cot_ref[g].astype(F32), 0.0).astype(BF16))
    joined = jnp.concatenate(
        [jnp.concatenate(own, axis=1), jnp.concatenate(other, axis=1)], axis=0
    )
    cotangent = jnp.concatenate(cot, axis=1)

    def times(weights, values):
        parts = jnp.dot(weights, values, preferred_element_type=F32)
        half = parts.shape[0] // 2
        return parts[:half] + parts[half:]

    pre = times(win_ref[...], joined) + bias_ref[:, 0:1]
    square = pre * pre
    bend = jnp.tanh(GELU_A * (pre + GELU_B * (square * pre)))
    hidden = 0.5 * pre * (1.0 + bend)
    slope = 0.5 * (1.0 + bend) + 0.5 * pre * (1.0 - bend * bend) * (
        GELU_A * (1.0 + (3.0 * GELU_B) * square)
    )
    grad_pre = (times(wout_t_ref[...], cotangent) * slope).astype(BF16)
    grad_joined = times(win_t_ref[...], grad_pre)
    for g in range(group):
        at = slice(g * KX, (g + 1) * KX)
        own_out[g] = grad_joined[:width, at].astype(BF16)
        other_out[g] = grad_joined[width:, at].astype(BF16)
    left = jnp.concatenate([grad_pre, cotangent], axis=0)
    ones = jnp.ones((width, group * KX), BF16)
    right = jnp.concatenate([joined, hidden.astype(BF16), ones], axis=0)
    sums_ref[...] += lax.dot_general(
        left, right, (((1,), (1,)), ((), ())), preferred_element_type=F32
    )


def mlp(slot0, kept, own, other, cot, win, bias, wout_t, win_t):
    slots, width, _ = own.shape
    group = 8
    while slots % group:
        group //= 2
    block = pl.BlockSpec((group, width, KX), lambda i: (i, 0, 0))
    scalar = pl.BlockSpec(memory_space=pltpu.SMEM)

    def whole(array):
        return pl.BlockSpec(array.shape, lambda i: (0, 0))

    return pl.pallas_call(
        functools.partial(mlp_kernel, slots, group, width),
        grid=(slots // group,),
        out_shape=(
            jax.ShapeDtypeStruct(own.shape, BF16),
            jax.ShapeDtypeStruct(own.shape, BF16),
            jax.ShapeDtypeStruct((2 * width, 4 * width), F32),
        ),
        in_specs=[
            scalar, scalar, block, block, block, whole(win), whole(bias), whole(wout_t), whole(win_t),
        ],
        out_specs=(block, block, pl.BlockSpec((2 * width, 4 * width), lambda i: (0, 0))),
        compiler_params=pltpu.CompilerParams(
            dimension_semantics=("arbitrary",), vmem_limit_bytes=32 << 20
        ),
        cost_estimate=pl.CostEstimate(
            flops=slots * KX * 2 * width * 16 * width,
            bytes_accessed=10 * own.size,
            transcendentals=slots * KX * width,
        ),
    )(slot0, kept, own, other, cot, win, bias, wout_t, win_t)


def split_rows(matrix):
    high = matrix.astype(BF16)
    low = (matrix - high.astype(F32)).astype(BF16)
    return jnp.concatenate([high, low], axis=0)


def block_matrix(blocks):
    count, m, n = blocks.shape
    if count == 1:
        return blocks[0]
    eye = jnp.eye(count, dtype=F32)
    return (blocks[:, :, None, :] * eye[:, None, :, None]).reshape(count * m, count * n)


def block_parts(matrix, count):
    rows, cols = matrix.shape
    split = matrix.reshape(count, rows // count, count, cols // count)
    return jnp.stack([split[b, :, b, :] for b in range(count)])


def local(fields, out_grads, partner, kept_blocks, weight_in, bias_in, weight_out):
    shards = lax.axis_size("row")
    channels, rows, n_cols = fields.shape[1:]
    n_rows = rows * shards
    count, bs = weight_out.shape[0], weight_out.shape[-1]
    own_rev = lax.axis_index("rev")
    row_rank = lax.axis_index("row")
    slots = KY // shards
    scale = 1.0 / math.sqrt(n_rows * n_cols)
    col_np = column_tables(n_cols)
    row_np = row_tables(n_rows, shards)
    col_table = jnp.asarray(col_np)
    row_table = lax.dynamic_index_in_dim(jnp.asarray(row_np), row_rank, 0, keepdims=False)
    inv_np = row_np.reshape(shards, 2, KY, rows).transpose(0, 1, 3, 2).reshape(shards, 2 * rows, KY)
    inv_table = lax.dynamic_index_in_dim(
        jnp.asarray(np.ascontiguousarray(inv_np)), row_rank, 0, keepdims=False
    )

    def spectrum(field):
        part = forward_partial(field, col_table, row_table, scale)
        return lax.psum_scatter(part, "row", scatter_dimension=0, tiled=True)

    spectra = spectrum(fields[0])
    grad_spec = spectrum(out_grads[0])
    target = partner[own_rev]

    def route(values):
        every = lax.all_gather(values, "rev", axis=0, tiled=False)
        return lax.dynamic_index_in_dim(every, target, 0, keepdims=False)

    own_real = block_matrix(weight_in[:, 0, :bs])
    own_imag = block_matrix(weight_in[:, 1, :bs])
    other_real = block_matrix(weight_in[:, 0, bs:])
    other_imag = block_matrix(weight_in[:, 1, bs:])
    out_real = block_matrix(weight_out[:, 0])
    out_imag = block_matrix(weight_out[:, 1])
    win_t = jnp.concatenate(
        [
            jnp.concatenate([own_real, own_imag], axis=1),
            jnp.concatenate([-own_imag, own_real], axis=1),
            jnp.concatenate([other_real, other_imag], axis=1),
            jnp.concatenate([-other_imag, other_real], axis=1),
        ],
        axis=0,
    )
    wout_t = jnp.concatenate(
        [
            jnp.concatenate([out_real, out_imag], axis=1),
            jnp.concatenate([-out_imag, out_real], axis=1),
        ],
        axis=0,
    )
    bias = jnp.concatenate([bias_in[:, 0].reshape(-1), bias_in[:, 1].reshape(-1)])
    bias = jnp.broadcast_to(bias[:, None], (2 * channels, KX))
    own_grads, other_grads, sums = mlp(
        (row_rank * slots).reshape(1).astype(jnp.int32),
        kept_blocks[own_rev].reshape(1),
        spectra,
        route(spectra),
        grad_spec,
        split_rows(win_t.T),
        bias,
        split_rows(wout_t),
        split_rows(win_t),
    )
    returned = route(other_grads)
    total = (own_grads.astype(F32) + returned.astype(F32)).astype(BF16)
    gathered = lax.all_gather(total, "row", axis=0, tiled=True)
    field_grads = inverse_field(gathered, inv_table, col_table.T, scale)

    summed = lax.psum(sums, ("rev", "row")) * (1.0 / math.sqrt(lax.axis_size("rev") * KX * KY))
    width = 2 * channels
    pre, cot = summed[:width], summed[width:]

    def complex_parts(grad):
        top, bottom = grad[:channels], grad[channels:]
        real = top[:, :channels] + bottom[:, channels:]
        imag = bottom[:, :channels] - top[:, channels:]
        return jnp.stack([block_parts(real.T, count), block_parts(imag.T, count)], axis=1)

    grad_win = jnp.concatenate(
        [complex_parts(pre[:, :width]), complex_parts(pre[:, width : 2 * width])], axis=2
    )
    grad_wout = complex_parts(cot[:, 2 * width : 3 * width])

    def bias_parts(column):
        return column.reshape(2, count, bs).transpose(1, 0, 2)

    return (
        field_grads[None],
        grad_win,
        bias_parts(pre[:, 3 * width]),
        grad_wout,
        bias_parts(cot[:, 3 * width]),
    )


def solution(mesh):
    placed = (P("rev", None, "row", None), P("rev", None, "row", None), P(), P(), P(), P(), P())
    return jax.shard_map(
        local,
        mesh=mesh,
        in_specs=placed,
        out_specs=(P("rev", None, "row", None), P(), P(), P(), P()),
        check_vma=False,
    )
```

```python
import functools
import math

import jax
import jax.numpy as jnp
import ml_dtypes
import numpy as np
from jax import lax
from jax.experimental import pallas as pl
from jax.experimental.pallas import tpu as pltpu
from jax.sharding import PartitionSpec as P

KX = 128
MB = 16
KY = 256
BF16 = jnp.bfloat16
F32 = jnp.float32
GELU_A = math.sqrt(2.0 / math.pi)
GELU_B = 0.044715


def column_tables(n_cols):
    phases = np.arange(n_cols)[:, None] * np.arange(KX)[None, :] % n_cols
    angles = phases.astype(np.float32) * np.float32(2.0 * math.pi / n_cols)
    both = np.concatenate([np.cos(angles), -np.sin(angles)], axis=1)
    return both.astype(ml_dtypes.bfloat16)


def row_tables(n_rows, shards):
    slot = np.arange(KY)
    signed = np.where(slot < KY // 2, slot, slot - KY + n_rows)
    phases = signed[:, None] * np.arange(n_rows)[None, :] % n_rows
    angles = phases.astype(np.float32) * np.float32(2.0 * math.pi / n_rows)
    both = np.concatenate([np.cos(angles), np.sin(angles)], axis=0)
    split = both.reshape(2 * KY, shards, n_rows // shards).transpose(1, 0, 2)
    return np.ascontiguousarray(split).astype(ml_dtypes.bfloat16)


def forward_kernel(channels, scale, x_ref, col_ref, row_ref, out_ref, held):
    step = pl.program_id(0)
    cols = jnp.dot(x_ref[0], col_ref[...], preferred_element_type=F32).astype(BF16)
    quads = jnp.dot(row_ref[...], cols, preferred_element_type=F32)
    real = (quads[:KY, :KX] + quads[KY:, KX:]) * scale
    imag = (quads[:KY, KX:] - quads[KY:, :KX]) * scale
    held[pl.ds(pl.multiple_of(step * KY, KY), KY), :] = real
    held[pl.ds(pl.multiple_of((channels + step) * KY, KY), KY), :] = imag

    @pl.when(step == channels - 1)
    def _():
        def turn(j, carry):
            out_ref[j] = held[pl.ds(j, 2 * channels, stride=KY), :].astype(BF16)
            return carry

        lax.fori_loop(0, KY, turn, 0, unroll=8)


def forward_partial(field, col_table, row_table, scale):
    channels, n_rows, n_cols = field.shape
    return pl.pallas_call(
        functools.partial(forward_kernel, channels, scale),
        grid=(channels,),
        out_shape=jax.ShapeDtypeStruct((KY, 2 * channels, KX), BF16),
        in_specs=[
            pl.BlockSpec((1, n_rows, n_cols), lambda c: (c, 0, 0)),
            pl.BlockSpec((n_cols, 2 * KX), lambda c: (0, 0)),
            pl.BlockSpec((2 * KY, n_rows), lambda c: (0, 0)),
        ],
        out_specs=pl.BlockSpec((KY, 2 * channels, KX), lambda c: (0, 0, 0)),
        scratch_shapes=[pltpu.VMEM((2 * channels * KY, KX), F32)],
        compiler_params=pltpu.CompilerParams(
            dimension_semantics=("arbitrary",), vmem_limit_bytes=32 << 20
        ),
        cost_estimate=pl.CostEstimate(
            flops=channels * n_rows * 2 * KX * (2 * n_cols + 4 * KY),
            bytes_accessed=2 * field.size + 4 * KY * channels * KX,
            transcendentals=0,
        ),
    )(field, col_table, row_table)


def inverse_kernel(channels, scale, total_ref, row_ref, col_ref, out_ref, held):
    step = pl.program_id(0)

    @pl.when(step == 0)
    def _():
        def turn(j, carry):
            at = pl.multiple_of(j * 2 * channels, 2 * channels)
            held[pl.ds(at, 2 * channels), :] = total_ref[j].astype(F32)
            return carry

        lax.fori_loop(0, KY, turn, 0, unroll=8)

    real = held[pl.ds(step, KY, stride=2 * channels), :].astype(BF16)
    imag = held[pl.ds(channels + step, KY, stride=2 * channels), :].astype(BF16)
    pair = jnp.concatenate([real, imag], axis=1)
    n_rows = out_ref.shape[1]
    quads = lax.dot_general(
        row_ref[...], pair, (((1,), (0,)), ((), ())), preferred_element_type=F32
    )
    rows_re = quads[:n_rows, :KX] - quads[n_rows:, KX:]
    rows_im = quads[n_rows:, :KX] + quads[:n_rows, KX:]
    rows = jnp.concatenate([rows_re, rows_im], axis=1).astype(BF16)
    field = jnp.dot(rows, col_ref[...], preferred_element_type=F32) * scale
    out_ref[0] = field.astype(BF16)


def inverse_field(total, row_table_t, col_table_t, scale):
    channels = total.shape[1] // 2
    n_rows, n_cols = row_table_t.shape[0] // 2, col_table_t.shape[1]
    return pl.pallas_call(
        functools.partial(inverse_kernel, channels, scale),
        grid=(channels,),
        out_shape=jax.ShapeDtypeStruct((channels, n_rows, n_cols), BF16),
        in_specs=[
            pl.BlockSpec((KY, 2 * channels, KX), lambda c: (0, 0, 0)),
            pl.BlockSpec((2 * n_rows, KY), lambda c: (0, 0)),
            pl.BlockSpec((2 * KX, n_cols), lambda c: (0, 0)),
        ],
        out_specs=pl.BlockSpec((1, n_rows, n_cols), lambda c: (c, 0, 0)),
        scratch_shapes=[pltpu.VMEM((2 * channels * KY, KX), F32)],
        compiler_params=pltpu.CompilerParams(
            dimension_semantics=("arbitrary",), vmem_limit_bytes=32 << 20
        ),
        cost_estimate=pl.CostEstimate(
            flops=channels * n_rows * 2 * KX * (2 * n_cols + 4 * KY),
            bytes_accessed=2 * channels * n_rows * n_cols + 4 * KY * channels * KX,
            transcendentals=0,
        ),
    )(total, row_table_t, col_table_t)


def mlp_kernel(
    slots, group, width, slot0_ref, kept_ref, own_ref, other_ref, cot_ref, win_ref, bias_ref,
    wout_t_ref, win_t_ref, own_out, other_out, sums_ref,
):
    step = pl.program_id(0)

    @pl.when(step == 0)
    def _():
        sums_ref[...] = jnp.zeros_like(sums_ref)

    lanes = lax.broadcasted_iota(jnp.int32, (width, KX), 1)
    limit = kept_ref[0] * MB
    own, other, cot = [], [], []
    for g in range(group):
        slot = slot0_ref[0] + step * group + g
        extent = jnp.where(slot < KY // 2, slot, KY - slot)
        keep = jnp.maximum(lanes, extent) < limit
        own.append(own_ref[g])
        other.append(other_ref[g])
        cot.append(jnp.where(keep, cot_ref[g].astype(F32), 0.0).astype(BF16))
    joined = jnp.concatenate(
        [jnp.concatenate(own, axis=1), jnp.concatenate(other, axis=1)], axis=0
    )
    cotangent = jnp.concatenate(cot, axis=1)

    def times(weights, values):
        parts = jnp.dot(weights, values, preferred_element_type=F32)
        half = parts.shape[0] // 2
        return parts[:half] + parts[half:]

    pre = times(win_ref[...], joined) + bias_ref[:, 0:1]
    square = pre * pre
    bend = jnp.tanh(GELU_A * (pre + GELU_B * (square * pre)))
    hidden = 0.5 * pre * (1.0 + bend)
    slope = 0.5 * (1.0 + bend) + 0.5 * pre * (1.0 - bend * bend) * (
        GELU_A * (1.0 + (3.0 * GELU_B) * square)
    )
    grad_pre = (times(wout_t_ref[...], cotangent) * slope).astype(BF16)
    grad_joined = times(win_t_ref[...], grad_pre)
    for g in range(group):
        at = slice(g * KX, (g + 1) * KX)
        own_out[g] = grad_joined[:width, at].astype(BF16)
        other_out[g] = grad_joined[width:, at].astype(BF16)
    left = jnp.concatenate([grad_pre, cotangent], axis=0)
    ones = jnp.ones((width, group * KX), BF16)
    right = jnp.concatenate([joined, hidden.astype(BF16), ones], axis=0)
    sums_ref[...] += lax.dot_general(
        left, right, (((1,), (1,)), ((), ())), preferred_element_type=F32
    )


def mlp(slot0, kept, own, other, cot, win, bias, wout_t, win_t):
    slots, width, _ = own.shape
    group = 8
    while slots % group:
        group //= 2
    block = pl.BlockSpec((group, width, KX), lambda i: (i, 0, 0))
    scalar = pl.BlockSpec(memory_space=pltpu.SMEM)

    def whole(array):
        return pl.BlockSpec(array.shape, lambda i: (0, 0))

    return pl.pallas_call(
        functools.partial(mlp_kernel, slots, group, width),
        grid=(slots // group,),
        out_shape=(
            jax.ShapeDtypeStruct(own.shape, BF16),
            jax.ShapeDtypeStruct(own.shape, BF16),
            jax.ShapeDtypeStruct((2 * width, 4 * width), F32),
        ),
        in_specs=[
            scalar, scalar, block, block, block, whole(win), whole(bias), whole(wout_t), whole(win_t),
        ],
        out_specs=(block, block, pl.BlockSpec((2 * width, 4 * width), lambda i: (0, 0))),
        compiler_params=pltpu.CompilerParams(
            dimension_semantics=("arbitrary",), vmem_limit_bytes=32 << 20
        ),
        cost_estimate=pl.CostEstimate(
            flops=slots * KX * 2 * width * 16 * width,
            bytes_accessed=10 * own.size,
            transcendentals=slots * KX * width,
        ),
    )(slot0, kept, own, other, cot, win, bias, wout_t, win_t)


MESH = pl.DeviceIdType.MESH


class Line:
    def __init__(self, size, send_sems, recv_sems):
        self.size, self.send_sems, self.recv_sems = size, send_sems, recv_sems
        self.me = lax.axis_index("row")

    def copy(self, side, tag, source, target):
        return pltpu.make_async_remote_copy(
            src_ref=source,
            dst_ref=target,
            send_sem=self.send_sems.at[side, tag],
            recv_sem=self.recv_sems.at[side, tag],
            device_id={"row": self.me + 1 - 2 * side},
            device_id_type=MESH,
        )


class Cube:
    def __init__(self, slots, send_sems, recv_sems):
        self.slots, self.send_sems, self.recv_sems = slots, send_sems, recv_sems
        self.me = lax.axis_index("rev")
        core, x, y = self.me % 2, (self.me // 2) % 2, self.me // 4
        self.step = {"c": 1 - 2 * core, "x": 2 - 4 * x, "y": 4 - 8 * y}

    def copy(self, tag, axis, slot, part=None):
        block = self.slots.at[slot]
        if part is not None:
            half = self.slots.shape[1] // 2
            block = self.slots.at[slot, pl.ds(part * half, half)]
        return pltpu.make_async_remote_copy(
            src_ref=block,
            dst_ref=block,
            send_sem=self.send_sems.at[tag],
            recv_sem=self.recv_sems.at[tag],
            device_id={"rev": self.me + self.step[axis]},
            device_id_type=MESH,
        )

    def numbered(self, tag):
        me, step = self.me, self.step
        axis, slot, part = (
            ("x", me, None),
            ("y", me, None),
            ("c", me, None),
            ("y", me + step["x"], 0),
            ("x", me + step["y"], 1),
            ("c", me + step["x"], None),
            ("c", me + step["y"], None),
            ("c", me + step["x"] + step["y"], None),
        )[tag]
        return self.copy(tag, axis, slot, part)

    def received(self, *tags):
        for tag in tags:
            self.numbered(tag).wait_recv()

    def start(self, *tags):
        for tag in tags:
            self.numbered(tag).start()

    def first(self):
        self.start(0, 1, 2)

    def second(self):
        self.received(0, 1)
        self.start(3, 4, 5, 6)

    def third(self):
        self.received(3, 4)
        self.start(7)

    def last(self):
        self.received(2, 5, 6, 7)
        for tag in range(8):
            self.numbered(tag).wait_send()


def greet(size, with_cube):
    me = lax.axis_index("row")
    barrier = pltpu.get_barrier_semaphore()
    sides = ((me < size - 1, me + 1), (me > 0, me - 1))
    for there, neighbour in sides:

        @pl.when(there)
        def _(neighbour=neighbour):
            pl.semaphore_signal(
                barrier, inc=1, device_id={"row": neighbour}, device_id_type=MESH
            )

    if with_cube:
        rev = lax.axis_index("rev")
        core, x, y = rev % 2, (rev // 2) % 2, rev // 4
        for other in (rev + 1 - 2 * core, rev + 2 - 4 * x, rev + 4 - 8 * y):
            pl.semaphore_signal(barrier, inc=1, device_id={"rev": other}, device_id_type=MESH)

    at_end = (me == 0) | (me == size - 1)
    around = 3 if with_cube else 0

    @pl.when(at_end)
    def _():
        pl.semaphore_wait(barrier, around + 1)

    @pl.when(jnp.logical_not(at_end))
    def _():
        pl.semaphore_wait(barrier, around + 2)


def add_into(held, side, slot, part_ref):
    held[side, slot] = (held[side, slot].astype(F32) + part_ref[slot].astype(F32)).astype(BF16)


def reduce_step(line, held, base, part_ref, t):
    n, me = line.size, line.me
    for side in (0, 1):
        place = me if side == 0 else n - 1 - me
        slot = n - 1 - t + me if side == 0 else t - (n - 1 - me)
        ahead = 1 if side == 0 else -1

        @pl.when((place <= t) & (place < n - 1))
        def _(side=side, place=place, slot=slot, ahead=ahead):
            copy = line.copy(side, base + slot, held.at[side, slot], held.at[side, slot])

            @pl.when(place > 0)
            def _():
                copy.wait_recv()
                add_into(held, side, slot, part_ref)

            @pl.when(place == 0)
            def _():
                held[side, slot] = part_ref[slot]

            @pl.when(place < t)
            def _():
                old = slot + ahead
                line.copy(side, base + old, held.at[side, old], held.at[side, old]).wait_send()

            copy.start()


def reduce_last(line, held, base, part_ref, out_ref):
    n, me = line.size, line.me
    for side in (0, 1):
        place = me if side == 0 else n - 1 - me
        ahead = 1 if side == 0 else -1

        @pl.when(place > 0)
        def _(side=side):
            line.copy(side, base + me, held.at[side, me], held.at[side, me]).wait_recv()

    @pl.when((me > 0) & (me < n - 1))
    def _():
        total = part_ref[me].astype(F32) + held[0, me].astype(F32) + held[1, me].astype(F32)
        out_ref[...] = total.astype(BF16)

    @pl.when(me == 0)
    def _():
        out_ref[...] = (part_ref[me].astype(F32) + held[1, me].astype(F32)).astype(BF16)

    @pl.when(me == n - 1)
    def _():
        out_ref[...] = (part_ref[me].astype(F32) + held[0, me].astype(F32)).astype(BF16)


def reduce_sent(line, held, base):
    n, me = line.size, line.me
    for side in (0, 1):
        place = me if side == 0 else n - 1 - me
        slot = me + 1 if side == 0 else me - 1

        @pl.when(place < n - 1)
        def _(side=side, slot=slot):
            line.copy(side, base + slot, held.at[side, slot], held.at[side, slot]).wait_send()


def exchange_kernel(
    n, revs, partner_ref, part_f, part_g, own_ref, other_ref, cot_ref, held_f, held_g, slots,
    line_send, line_recv, cube_send, cube_recv,
):
    greet(n, True)
    line = Line(n, line_send, line_recv)
    cube = Cube(slots, cube_send, cube_recv)
    for t in range(n - 1):
        reduce_step(line, held_f, 0, part_f, t)
    reduce_last(line, held_f, 0, part_f, own_ref)
    slots[cube.me] = own_ref[...]
    cube.first()
    reduce_sent(line, held_f, 0)
    for t in range(n - 1):
        reduce_step(line, held_g, n, part_g, t)
        if t == 0:
            cube.second()
        if t == 1:
            cube.third()
    if n < 3:
        cube.third()
    reduce_last(line, held_g, n, part_g, cot_ref)
    reduce_sent(line, held_g, n)
    cube.last()
    other_ref[...] = slots[partner_ref[cube.me]]


def exchange(part_f, part_g, partner, shards, revs):
    slots, width = part_f.shape[0] // shards, part_f.shape[1]
    block = (slots, width, KX)
    vmem = pl.BlockSpec(memory_space=pltpu.VMEM)
    shape = jax.ShapeDtypeStruct(block, BF16)
    return pl.pallas_call(
        functools.partial(exchange_kernel, shards, revs),
        out_shape=(shape, shape, shape),
        in_specs=[pl.BlockSpec(memory_space=pltpu.SMEM), vmem, vmem],
        out_specs=(vmem, vmem, vmem),
        scratch_shapes=[
            pltpu.VMEM((2, shards) + block, BF16),
            pltpu.VMEM((2, shards) + block, BF16),
            pltpu.VMEM((revs,) + block, BF16),
            pltpu.SemaphoreType.DMA((2, 2 * shards)),
            pltpu.SemaphoreType.DMA((2, 2 * shards)),
            pltpu.SemaphoreType.DMA((8,)),
            pltpu.SemaphoreType.DMA((8,)),
        ],
        compiler_params=pltpu.CompilerParams(
            collective_id=0, has_side_effects=True, vmem_limit_bytes=40 << 20
        ),
    )(partner, part_f.reshape((shards,) + block), part_g.reshape((shards,) + block))


def finish_kernel(
    n, revs, partner_ref, own_ref, other_ref, sums_ref, all_ref, total_ref, slots, gathered,
    small, small_rows, line_send, line_recv, cube_send, cube_recv, small_send, small_recv,
):
    greet(n, True)
    line = Line(n, line_send, line_recv)
    cube = Cube(slots, cube_send, cube_recv)
    rev, me = cube.me, line.me
    slots[rev] = other_ref[...]
    cube.first()
    small[0] = sums_ref[...]
    for i, axis in enumerate(("x", "y", "c")):
        copy = pltpu.make_async_remote_copy(
            src_ref=small.at[i],
            dst_ref=small.at[4 + i],
            send_sem=small_send.at[i],
            recv_sem=small_recv.at[i],
            device_id={"rev": rev + cube.step[axis]},
            device_id_type=MESH,
        )
        copy.start()
        copy.wait_recv()
        small[i + 1] = small[i] + small[4 + i]
        copy.wait_send()
    small_rows[me] = small[3]
    cube.second()
    cube.third()
    cube.last()
    total = own_ref[...].astype(F32) + slots[partner_ref[rev]].astype(F32)
    gathered[me] = total.astype(BF16)
    for t in range(n):
        for side in (0, 1):
            place = me if side == 0 else n - 1 - me
            slot = me - t if side == 0 else me + t
            old = me - t + 1 if side == 0 else me + t - 1
            if t > 0:

                @pl.when(place >= t)
                def _(side=side, slot=slot):
                    line.copy(side, slot, gathered.at[slot], gathered.at[slot]).wait_recv()
                    line.copy(
                        side, n + slot, small_rows.at[slot], small_rows.at[slot]
                    ).wait_recv()

                @pl.when((place >= t - 1) & (place < n - 1))
                def _(side=side, old=old):
                    line.copy(side, old, gathered.at[old], gathered.at[old]).wait_send()
                    line.copy(side, n + old, small_rows.at[old], small_rows.at[old]).wait_send()

            if t < n - 1:

                @pl.when((place >= t) & (place < n - 1))
                def _(side=side, slot=slot):
                    line.copy(side, n + slot, small_rows.at[slot], small_rows.at[slot]).start()
                    line.copy(side, slot, gathered.at[slot], gathered.at[slot]).start()

    all_ref[...] = gathered[...]
    summed = small_rows[0]
    for i in range(1, n):
        summed = summed + small_rows[i]
    total_ref[...] = summed


def finish(own, other, sums, partner, shards, revs):
    vmem = pl.BlockSpec(memory_space=pltpu.VMEM)
    gathered, summed = pl.pallas_call(
        functools.partial(finish_kernel, shards, revs),
        out_shape=(
            jax.ShapeDtypeStruct((shards,) + own.shape, BF16),
            jax.ShapeDtypeStruct(sums.shape, F32),
        ),
        in_specs=[pl.BlockSpec(memory_space=pltpu.SMEM), vmem, vmem, vmem],
        out_specs=(vmem, vmem),
        scratch_shapes=[
            pltpu.VMEM((revs,) + own.shape, BF16),
            pltpu.VMEM((shards,) + own.shape, BF16),
            pltpu.VMEM((7,) + sums.shape, F32),
            pltpu.VMEM((shards,) + sums.shape, F32),
            pltpu.SemaphoreType.DMA((2, 2 * shards)),
            pltpu.SemaphoreType.DMA((2, 2 * shards)),
            pltpu.SemaphoreType.DMA((8,)),
            pltpu.SemaphoreType.DMA((8,)),
            pltpu.SemaphoreType.DMA((3,)),
            pltpu.SemaphoreType.DMA((3,)),
        ],
        compiler_params=pltpu.CompilerParams(
            collective_id=1, has_side_effects=True, vmem_limit_bytes=40 << 20
        ),
    )(partner, own, other, sums)
    return gathered.reshape((shards * own.shape[0],) + own.shape[1:]), summed


def split_rows(matrix):
    high = matrix.astype(BF16)
    low = (matrix - high.astype(F32)).astype(BF16)
    return jnp.concatenate([high, low], axis=0)


def block_matrix(blocks):
    count, m, n = blocks.shape
    if count == 1:
        return blocks[0]
    eye = jnp.eye(count, dtype=F32)
    return (blocks[:, :, None, :] * eye[:, None, :, None]).reshape(count * m, count * n)


def block_parts(matrix, count):
    rows, cols = matrix.shape
    split = matrix.reshape(count, rows // count, count, cols // count)
    return jnp.stack([split[b, :, b, :] for b in range(count)])


def local(fields, out_grads, partner, kept_blocks, weight_in, bias_in, weight_out):
    shards = lax.axis_size("row")
    channels, rows, n_cols = fields.shape[1:]
    n_rows = rows * shards
    count, bs = weight_out.shape[0], weight_out.shape[-1]
    own_rev = lax.axis_index("rev")
    row_rank = lax.axis_index("row")
    slots = KY // shards
    scale = 1.0 / math.sqrt(n_rows * n_cols)
    col_np = column_tables(n_cols)
    row_np = row_tables(n_rows, shards)
    col_table = jnp.asarray(col_np)
    row_table = lax.dynamic_index_in_dim(jnp.asarray(row_np), row_rank, 0, keepdims=False)
    inv_np = row_np.reshape(shards, 2, KY, rows).transpose(0, 1, 3, 2).reshape(shards, 2 * rows, KY)
    inv_table = lax.dynamic_index_in_dim(
        jnp.asarray(np.ascontiguousarray(inv_np)), row_rank, 0, keepdims=False
    )

    revs = lax.axis_size("rev")
    part_f = forward_partial(fields[0], col_table, row_table, scale)
    part_g = forward_partial(out_grads[0], col_table, row_table, scale)
    target = partner[own_rev]

    def route(values):
        every = lax.all_gather(values, "rev", axis=0, tiled=False)
        return lax.dynamic_index_in_dim(every, target, 0, keepdims=False)

    own_kernels = revs == 8 and shards > 1
    if own_kernels:
        spectra, other, grad_spec = exchange(part_f, part_g, partner, shards, revs)
    else:
        spectra, grad_spec = (
            lax.psum_scatter(part, "row", scatter_dimension=0, tiled=True)
            for part in (part_f, part_g)
        )
        other = route(spectra)

    own_real = block_matrix(weight_in[:, 0, :bs])
    own_imag = block_matrix(weight_in[:, 1, :bs])
    other_real = block_matrix(weight_in[:, 0, bs:])
    other_imag = block_matrix(weight_in[:, 1, bs:])
    out_real = block_matrix(weight_out[:, 0])
    out_imag = block_matrix(weight_out[:, 1])
    win_t = jnp.concatenate(
        [
            jnp.concatenate([own_real, own_imag], axis=1),
            jnp.concatenate([-own_imag, own_real], axis=1),
            jnp.concatenate([other_real, other_imag], axis=1),
            jnp.concatenate([-other_imag, other_real], axis=1),
        ],
        axis=0,
    )
    wout_t = jnp.concatenate(
        [
            jnp.concatenate([out_real, out_imag], axis=1),
            jnp.concatenate([-out_imag, out_real], axis=1),
        ],
        axis=0,
    )
    bias = jnp.concatenate([bias_in[:, 0].reshape(-1), bias_in[:, 1].reshape(-1)])
    bias = jnp.broadcast_to(bias[:, None], (2 * channels, KX))
    own_grads, other_grads, sums = mlp(
        (row_rank * slots).reshape(1).astype(jnp.int32),
        kept_blocks[own_rev].reshape(1),
        spectra,
        other,
        grad_spec,
        split_rows(win_t.T),
        bias,
        split_rows(wout_t),
        split_rows(win_t),
    )
    if own_kernels:
        gathered, summed = finish(own_grads, other_grads, sums, partner, shards, revs)
    else:
        total = own_grads.astype(F32) + route(other_grads).astype(F32)
        gathered = lax.all_gather(total.astype(BF16), "row", axis=0, tiled=True)
        summed = lax.psum(sums, ("rev", "row"))
    field_grads = inverse_field(gathered, inv_table, col_table.T, scale)

    summed = summed * (1.0 / math.sqrt(revs * KX * KY))
    width = 2 * channels
    pre, cot = summed[:width], summed[width:]

    def complex_parts(grad):
        top, bottom = grad[:channels], grad[channels:]
        real = top[:, :channels] + bottom[:, channels:]
        imag = bottom[:, :channels] - top[:, channels:]
        return jnp.stack([block_parts(real.T, count), block_parts(imag.T, count)], axis=1)

    grad_win = jnp.concatenate(
        [complex_parts(pre[:, :width]), complex_parts(pre[:, width : 2 * width])], axis=2
    )
    grad_wout = complex_parts(cot[:, 2 * width : 3 * width])

    def bias_parts(column):
        return column.reshape(2, count, bs).transpose(1, 0, 2)

    return (
        field_grads[None],
        grad_win,
        bias_parts(pre[:, 3 * width]),
        grad_wout,
        bias_parts(cot[:, 3 * width]),
    )


def solution(mesh):
    placed = (P("rev", None, "row", None), P("rev", None, "row", None), P(), P(), P(), P(), P())
    return jax.shard_map(
        local,
        mesh=mesh,
        in_specs=placed,
        out_specs=(P("rev", None, "row", None), P(), P(), P(), P()),
        check_vma=False,
    )
```

```python
import functools
import math

import jax
import jax.numpy as jnp
import ml_dtypes
import numpy as np
from jax import lax
from jax.experimental import pallas as pl
from jax.experimental.pallas import tpu as pltpu
from jax.sharding import PartitionSpec as P

KX = 128
MB = 16
KY = 256
BF16 = jnp.bfloat16
F32 = jnp.float32
GELU_A = math.sqrt(2.0 / math.pi)
GELU_B = 0.044715


def column_tables(n_cols):
    phases = np.arange(n_cols)[:, None] * np.arange(KX)[None, :] % n_cols
    angles = phases.astype(np.float32) * np.float32(2.0 * math.pi / n_cols)
    both = np.concatenate([np.cos(angles), -np.sin(angles)], axis=1)
    return both.astype(ml_dtypes.bfloat16)


def row_tables(n_rows, shards):
    slot = np.arange(KY)
    signed = np.where(slot < KY // 2, slot, slot - KY + n_rows)
    phases = signed[:, None] * np.arange(n_rows)[None, :] % n_rows
    angles = phases.astype(np.float32) * np.float32(2.0 * math.pi / n_rows)
    both = np.concatenate([np.cos(angles), np.sin(angles)], axis=0)
    split = both.reshape(2 * KY, shards, n_rows // shards).transpose(1, 0, 2)
    return np.ascontiguousarray(split).astype(ml_dtypes.bfloat16)


def forward_channel(channels, scale, values, col_ref, row_ref, held, channel):
    cols = jnp.dot(values, col_ref[...], preferred_element_type=F32).astype(BF16)
    quads = jnp.dot(row_ref[...], cols, preferred_element_type=F32)
    real = (quads[:KY, :KX] + quads[KY:, KX:]) * scale
    imag = (quads[:KY, KX:] - quads[KY:, :KX]) * scale
    held[pl.ds(pl.multiple_of(channel * KY, KY), KY), :] = real
    held[pl.ds(pl.multiple_of((channels + channel) * KY, KY), KY), :] = imag


def forward_kernel(channels, group, scale, x_ref, col_ref, row_ref, out_ref, held):
    step = pl.program_id(0)
    for i in range(group):
        forward_channel(channels, scale, x_ref[i], col_ref, row_ref, held, step * group + i)

    @pl.when(step == channels // group - 1)
    def _():
        def turn(j, carry):
            out_ref[j] = held[pl.ds(j, 2 * channels, stride=KY), :].astype(BF16)
            return carry

        lax.fori_loop(0, KY, turn, 0, unroll=8)


def forward_partial(field, col_table, row_table, scale):
    channels, n_rows, n_cols = field.shape
    group = 2 if channels % 2 == 0 else 1
    return pl.pallas_call(
        functools.partial(forward_kernel, channels, group, scale),
        grid=(channels // group,),
        out_shape=jax.ShapeDtypeStruct((KY, 2 * channels, KX), BF16),
        in_specs=[
            pl.BlockSpec((group, n_rows, n_cols), lambda c: (c, 0, 0)),
            pl.BlockSpec((n_cols, 2 * KX), lambda c: (0, 0)),
            pl.BlockSpec((2 * KY, n_rows), lambda c: (0, 0)),
        ],
        out_specs=pl.BlockSpec((KY, 2 * channels, KX), lambda c: (0, 0, 0)),
        scratch_shapes=[pltpu.VMEM((2 * channels * KY, KX), F32)],
        compiler_params=pltpu.CompilerParams(
            dimension_semantics=("arbitrary",), vmem_limit_bytes=57 << 20
        ),
        cost_estimate=pl.CostEstimate(
            flops=channels * n_rows * 2 * KX * (2 * n_cols + 4 * KY),
            bytes_accessed=2 * field.size + 4 * KY * channels * KX,
            transcendentals=0,
        ),
    )(field, col_table, row_table)


def inverse_kernel(channels, scale, total_ref, row_ref, col_ref, out_ref, held):
    step = pl.program_id(0)

    @pl.when(step == 0)
    def _():
        def turn(j, carry):
            at = pl.multiple_of(j * 2 * channels, 2 * channels)
            held[pl.ds(at, 2 * channels), :] = total_ref[j].astype(F32)
            return carry

        lax.fori_loop(0, KY, turn, 0, unroll=8)

    for i in range(out_ref.shape[0]):
        channel = step * out_ref.shape[0] + i
        real = held[pl.ds(channel, KY, stride=2 * channels), :].astype(BF16)
        imag = held[pl.ds(channels + channel, KY, stride=2 * channels), :].astype(BF16)
        pair = jnp.concatenate([real, imag], axis=1)
        n_rows = out_ref.shape[1]
        quads = lax.dot_general(
            row_ref[...], pair, (((1,), (0,)), ((), ())), preferred_element_type=F32
        )
        rows_re = quads[:n_rows, :KX] - quads[n_rows:, KX:]
        rows_im = quads[n_rows:, :KX] + quads[:n_rows, KX:]
        rows = jnp.concatenate([rows_re, rows_im], axis=1).astype(BF16)
        field = jnp.dot(rows, col_ref[...], preferred_element_type=F32) * scale
        out_ref[i] = field.astype(BF16)


def inverse_field(total, row_table_t, col_table_t, scale):
    channels = total.shape[1] // 2
    n_rows, n_cols = row_table_t.shape[0] // 2, col_table_t.shape[1]
    group = 2 if channels % 2 == 0 else 1
    return pl.pallas_call(
        functools.partial(inverse_kernel, channels, scale),
        grid=(channels // group,),
        out_shape=jax.ShapeDtypeStruct((channels, n_rows, n_cols), BF16),
        in_specs=[
            pl.BlockSpec((KY, 2 * channels, KX), lambda c: (0, 0, 0)),
            pl.BlockSpec((2 * n_rows, KY), lambda c: (0, 0)),
            pl.BlockSpec((2 * KX, n_cols), lambda c: (0, 0)),
        ],
        out_specs=pl.BlockSpec((group, n_rows, n_cols), lambda c: (c, 0, 0)),
        scratch_shapes=[pltpu.VMEM((2 * channels * KY, KX), F32)],
        compiler_params=pltpu.CompilerParams(
            dimension_semantics=("arbitrary",), vmem_limit_bytes=32 << 20
        ),
        cost_estimate=pl.CostEstimate(
            flops=channels * n_rows * 2 * KX * (2 * n_cols + 4 * KY),
            bytes_accessed=2 * channels * n_rows * n_cols + 4 * KY * channels * KX,
            transcendentals=0,
        ),
    )(total, row_table_t, col_table_t)


def mlp_kernel(
    slots, group, width, slot0_ref, kept_ref, own_ref, other_ref, cot_ref, win_ref, bias_ref,
    wout_t_ref, win_t_ref, own_out, other_out, sums_ref,
):
    step = pl.program_id(0)

    @pl.when(step == 0)
    def _():
        sums_ref[...] = jnp.zeros_like(sums_ref)

    lanes = lax.broadcasted_iota(jnp.int32, (width, KX), 1)
    limit = kept_ref[0] * MB
    own, other, cot = [], [], []
    for g in range(group):
        slot = slot0_ref[0] + step * group + g
        extent = jnp.where(slot < KY // 2, slot, KY - slot)
        keep = jnp.maximum(lanes, extent) < limit
        own.append(own_ref[g])
        other.append(other_ref[g])
        cot.append(jnp.where(keep, cot_ref[g].astype(F32), 0.0).astype(BF16))
    joined = jnp.concatenate(
        [jnp.concatenate(own, axis=1), jnp.concatenate(other, axis=1)], axis=0
    )
    cotangent = jnp.concatenate(cot, axis=1)

    def times(weights, values):
        parts = jnp.dot(weights, values, preferred_element_type=F32)
        half = parts.shape[0] // 2
        return parts[:half] + parts[half:]

    pre = times(win_ref[...], joined) + bias_ref[:, 0:1]
    square = pre * pre
    bend = jnp.tanh(GELU_A * (pre + GELU_B * (square * pre)))
    hidden = 0.5 * pre * (1.0 + bend)
    slope = 0.5 * (1.0 + bend) + 0.5 * pre * (1.0 - bend * bend) * (
        GELU_A * (1.0 + (3.0 * GELU_B) * square)
    )
    grad_pre = (times(wout_t_ref[...], cotangent) * slope).astype(BF16)
    grad_joined = times(win_t_ref[...], grad_pre)
    for g in range(group):
        at = slice(g * KX, (g + 1) * KX)
        own_out[g] = grad_joined[:width, at].astype(BF16)
        other_out[g] = grad_joined[width:, at].astype(BF16)
    left = jnp.concatenate([grad_pre, cotangent], axis=0)
    ones = jnp.ones((width, group * KX), BF16)
    right = jnp.concatenate([joined, hidden.astype(BF16), ones], axis=0)
    sums_ref[...] += lax.dot_general(
        left, right, (((1,), (1,)), ((), ())), preferred_element_type=F32
    )


def mlp(slot0, kept, own, other, cot, win, bias, wout_t, win_t):
    slots, width, _ = own.shape
    group = 8
    while slots % group:
        group //= 2
    block = pl.BlockSpec((group, width, KX), lambda i: (i, 0, 0))
    scalar = pl.BlockSpec(memory_space=pltpu.SMEM)

    def whole(array):
        return pl.BlockSpec(array.shape, lambda i: (0, 0))

    return pl.pallas_call(
        functools.partial(mlp_kernel, slots, group, width),
        grid=(slots // group,),
        out_shape=(
            jax.ShapeDtypeStruct(own.shape, BF16),
            jax.ShapeDtypeStruct(own.shape, BF16),
            jax.ShapeDtypeStruct((2 * width, 4 * width), F32),
        ),
        in_specs=[
            scalar, scalar, block, block, block, whole(win), whole(bias), whole(wout_t), whole(win_t),
        ],
        out_specs=(block, block, pl.BlockSpec((2 * width, 4 * width), lambda i: (0, 0))),
        compiler_params=pltpu.CompilerParams(
            dimension_semantics=("arbitrary",), vmem_limit_bytes=32 << 20
        ),
        cost_estimate=pl.CostEstimate(
            flops=slots * KX * 2 * width * 16 * width,
            bytes_accessed=10 * own.size,
            transcendentals=slots * KX * width,
        ),
    )(slot0, kept, own, other, cot, win, bias, wout_t, win_t)


MESH = pl.DeviceIdType.MESH


class Line:
    def __init__(self, size, send_sems, recv_sems):
        self.size, self.send_sems, self.recv_sems = size, send_sems, recv_sems
        self.me = lax.axis_index("row")

    def copy(self, side, tag, source, target):
        return pltpu.make_async_remote_copy(
            src_ref=source,
            dst_ref=target,
            send_sem=self.send_sems.at[side, tag],
            recv_sem=self.recv_sems.at[side, tag],
            device_id={"row": self.me + 1 - 2 * side},
            device_id_type=MESH,
        )


class Cube:
    def __init__(self, slots, send_sems, recv_sems, base=0):
        self.slots, self.send_sems, self.recv_sems = slots, send_sems, recv_sems
        self.base = base
        self.me = lax.axis_index("rev")
        core, x, y = self.me % 2, (self.me // 2) % 2, self.me // 4
        self.step = {"c": 1 - 2 * core, "x": 2 - 4 * x, "y": 4 - 8 * y}

    def copy(self, tag, axis, slot, part=None):
        block = self.slots.at[slot]
        if part is not None:
            half = self.slots.shape[1] // 2
            block = self.slots.at[slot, pl.ds(part * half, half)]
        return pltpu.make_async_remote_copy(
            src_ref=block,
            dst_ref=block,
            send_sem=self.send_sems.at[self.base + tag],
            recv_sem=self.recv_sems.at[self.base + tag],
            device_id={"rev": self.me + self.step[axis]},
            device_id_type=MESH,
        )

    def numbered(self, tag):
        me, step = self.me, self.step
        axis, slot, part = (
            ("x", me, None),
            ("y", me, None),
            ("c", me, None),
            ("y", me + step["x"], 0),
            ("x", me + step["y"], 1),
            ("c", me + step["x"], None),
            ("c", me + step["y"], None),
            ("c", me + step["x"] + step["y"], None),
        )[tag]
        return self.copy(tag, axis, slot, part)

    def received(self, *tags):
        for tag in tags:
            self.numbered(tag).wait_recv()

    def start(self, *tags):
        for tag in tags:
            self.numbered(tag).start()

    def first(self):
        self.start(0, 1, 2)

    def second(self):
        self.received(0, 1)
        self.start(3, 4, 5, 6)

    def third(self):
        self.received(3, 4)
        self.start(7)

    def last(self):
        self.received(2, 5, 6, 7)
        for tag in range(8):
            self.numbered(tag).wait_send()


def greet(size, with_cube):
    me = lax.axis_index("row")
    barrier = pltpu.get_barrier_semaphore()
    sides = ((me < size - 1, me + 1), (me > 0, me - 1))
    for there, neighbour in sides:

        @pl.when(there)
        def _(neighbour=neighbour):
            pl.semaphore_signal(
                barrier, inc=1, device_id={"row": neighbour}, device_id_type=MESH
            )

    if with_cube:
        rev = lax.axis_index("rev")
        core, x, y = rev % 2, (rev // 2) % 2, rev // 4
        for other in (rev + 1 - 2 * core, rev + 2 - 4 * x, rev + 4 - 8 * y):
            pl.semaphore_signal(barrier, inc=1, device_id={"rev": other}, device_id_type=MESH)

    at_end = (me == 0) | (me == size - 1)
    around = 3 if with_cube else 0

    @pl.when(at_end)
    def _():
        pl.semaphore_wait(barrier, around + 1)

    @pl.when(jnp.logical_not(at_end))
    def _():
        pl.semaphore_wait(barrier, around + 2)


def add_into(held, side, slot, part_ref):
    held[side, slot] = (held[side, slot].astype(F32) + part_ref[slot].astype(F32)).astype(BF16)


def reduce_step(line, held, base, part_ref, t):
    n, me = line.size, line.me
    for side in (0, 1):
        place = me if side == 0 else n - 1 - me
        slot = n - 1 - t + me if side == 0 else t - (n - 1 - me)
        ahead = 1 if side == 0 else -1

        @pl.when((place <= t) & (place < n - 1))
        def _(side=side, place=place, slot=slot, ahead=ahead):
            copy = line.copy(side, base + slot, held.at[side, slot], held.at[side, slot])

            @pl.when(place > 0)
            def _():
                copy.wait_recv()
                add_into(held, side, slot, part_ref)

            @pl.when(place == 0)
            def _():
                held[side, slot] = part_ref[slot]

            @pl.when(place < t)
            def _():
                old = slot + ahead
                line.copy(side, base + old, held.at[side, old], held.at[side, old]).wait_send()

            copy.start()


def reduce_last(line, held, base, part_ref, out_ref):
    n, me = line.size, line.me
    for side in (0, 1):
        place = me if side == 0 else n - 1 - me
        ahead = 1 if side == 0 else -1

        @pl.when(place > 0)
        def _(side=side):
            line.copy(side, base + me, held.at[side, me], held.at[side, me]).wait_recv()

    @pl.when((me > 0) & (me < n - 1))
    def _():
        total = part_ref[me].astype(F32) + held[0, me].astype(F32) + held[1, me].astype(F32)
        out_ref[...] = total.astype(BF16)

    @pl.when(me == 0)
    def _():
        out_ref[...] = (part_ref[me].astype(F32) + held[1, me].astype(F32)).astype(BF16)

    @pl.when(me == n - 1)
    def _():
        out_ref[...] = (part_ref[me].astype(F32) + held[0, me].astype(F32)).astype(BF16)


def reduce_sent(line, held, base):
    n, me = line.size, line.me
    for side in (0, 1):
        place = me if side == 0 else n - 1 - me
        slot = me + 1 if side == 0 else me - 1

        @pl.when(place < n - 1)
        def _(side=side, slot=slot):
            line.copy(side, base + slot, held.at[side, slot], held.at[side, slot]).wait_send()


def exchange_kernel(
    n, channels, scale, partner_ref, part_f, field_ref, col_ref, row_ref, own_ref, other_ref,
    cot_ref, held_f, held_g, slots, field, spread, part_g, line_send, line_recv, cube_send,
    cube_recv, field_sem,
):
    fetch = pltpu.make_async_copy(field_ref, field, field_sem)
    fetch.start()
    greet(n, True)
    line = Line(n, line_send, line_recv)
    cube = Cube(slots, cube_send, cube_recv)

    def transform(channel, carry):
        forward_channel(channels, scale, field[channel], col_ref, row_ref, spread, channel)
        return carry

    for t in range(n - 1):
        reduce_step(line, held_f, 0, part_f, t)
        if t == 0:
            fetch.wait()
        lax.fori_loop(channels * t // (n - 1), channels * (t + 1) // (n - 1), transform, 0)
    rows = KY // n
    for shard in range(n):

        def turn(j, carry, shard=shard):
            values = spread[pl.ds(shard * rows + j, 2 * channels, stride=KY), :]
            part_g[shard, j] = values.astype(BF16)
            return carry

        lax.fori_loop(0, rows, turn, 0, unroll=8)
    reduce_last(line, held_f, 0, part_f, own_ref)
    slots[cube.me] = own_ref[...]
    reduce_sent(line, held_f, 0)
    cube.first()
    for t in range(n - 1):
        reduce_step(line, held_g, n, part_g, t)
        if t == 0:
            cube.second()
        if t == 1:
            cube.third()
    if n < 3:
        cube.third()
    reduce_last(line, held_g, n, part_g, cot_ref)
    reduce_sent(line, held_g, n)
    cube.last()
    other_ref[...] = slots[partner_ref[cube.me]]


def exchange(part_f, field_g, col_table, row_table, partner, shards, revs, scale):
    slots, width = part_f.shape[0] // shards, part_f.shape[1]
    block = (slots, width, KX)
    vmem = pl.BlockSpec(memory_space=pltpu.VMEM)
    shape = jax.ShapeDtypeStruct(block, BF16)
    return pl.pallas_call(
        functools.partial(exchange_kernel, shards, width // 2, scale),
        out_shape=(shape, shape, shape),
        in_specs=[
            pl.BlockSpec(memory_space=pltpu.SMEM), vmem, pl.BlockSpec(memory_space=pl.ANY), vmem, vmem,
        ],
        out_specs=(vmem, vmem, vmem),
        scratch_shapes=[
            pltpu.VMEM((2, shards) + block, BF16),
            pltpu.VMEM((2, shards) + block, BF16),
            pltpu.VMEM((revs,) + block, BF16),
            pltpu.VMEM(field_g.shape, BF16),
            pltpu.VMEM((width * KY, KX), F32),
            pltpu.VMEM((shards,) + block, BF16),
            pltpu.SemaphoreType.DMA((2, 2 * shards)),
            pltpu.SemaphoreType.DMA((2, 2 * shards)),
            pltpu.SemaphoreType.DMA((8,)),
            pltpu.SemaphoreType.DMA((8,)),
            pltpu.SemaphoreType.DMA,
        ],
        compiler_params=pltpu.CompilerParams(
            collective_id=0, has_side_effects=True, vmem_limit_bytes=57 << 20
        ),
    )(partner, part_f.reshape((shards,) + block), field_g, col_table, row_table)


def finish_kernel(
    n, revs, partner_ref, own_ref, other_ref, sums_ref, all_ref, total_ref, slots_a,
    slots_b, gathered, small, small_rows, line_send, line_recv, cube_send, cube_recv, small_send, small_recv,
):
    greet(n, True)
    line = Line(n, line_send, line_recv)
    half = own_ref.shape[0] // 2
    buffers = (slots_a, slots_b)
    cubes = [Cube(buffers[h], cube_send, cube_recv, 8 * h) for h in (0, 1)]
    rev, me = cubes[0].me, line.me
    for h in (0, 1):
        buffers[h][rev] = other_ref[h * half : (h + 1) * half]
    small[0] = sums_ref[...]

    def small_copy(i):
        return pltpu.make_async_remote_copy(
            src_ref=small.at[i],
            dst_ref=small.at[4 + i],
            send_sem=small_send.at[i],
            recv_sem=small_recv.at[i],
            device_id={"rev": rev + cubes[0].step["xyc"[i]]},
            device_id_type=MESH,
        )

    def small_add(i):
        small_copy(i).wait_recv()
        small[i + 1] = small[i] + small[4 + i]

    def add_half(h):
        part = pl.ds(h * half, half)
        other = buffers[h][partner_ref[rev]]
        gathered[me, part] = (own_ref[part].astype(F32) + other.astype(F32)).astype(BF16)

    def row_copies(side, slot, h):
        block = gathered.at[slot, pl.ds(h * half, half)]
        copies = [line.copy(side, h * n + slot, block, block)]
        if h == 0:
            few = small_rows.at[slot]
            copies.insert(0, line.copy(side, 2 * n + slot, few, few))
        return copies

    def row_step(t, h):
        for side in (0, 1):
            place = me if side == 0 else n - 1 - me
            slot = me - t if side == 0 else me + t
            old = me - t + 1 if side == 0 else me + t - 1
            if t > 0:

                @pl.when(place >= t)
                def _(side=side, slot=slot):
                    for copy in row_copies(side, slot, h):
                        copy.wait_recv()

                @pl.when((place >= t - 1) & (place < n - 1))
                def _(side=side, old=old):
                    for copy in row_copies(side, old, h):
                        copy.wait_send()

            if t < n - 1:

                @pl.when((place >= t) & (place < n - 1))
                def _(side=side, slot=slot):
                    for copy in row_copies(side, slot, h):
                        copy.start()

    small_copy(0).start()
    cubes[0].first()
    small_add(0)
    small_copy(1).start()
    cubes[0].second()
    cubes[1].first()
    small_add(1)
    small_copy(2).start()
    cubes[0].third()
    small_add(2)
    small_rows[me] = small[3]
    cubes[0].last()
    for i in range(3):
        small_copy(i).wait_send()
    add_half(0)
    row_step(0, 0)
    cubes[1].second()
    cubes[1].third()
    cubes[1].last()
    add_half(1)
    row_step(0, 1)
    for t in range(1, n):
        row_step(t, 0)
        row_step(t, 1)

    all_ref[...] = gathered[...]
    summed = small_rows[0]
    for i in range(1, n):
        summed = summed + small_rows[i]
    total_ref[...] = summed


def finish(own, other, sums, partner, shards, revs):
    vmem = pl.BlockSpec(memory_space=pltpu.VMEM)
    gathered, summed = pl.pallas_call(
        functools.partial(finish_kernel, shards, revs),
        out_shape=(
            jax.ShapeDtypeStruct((shards,) + own.shape, BF16),
            jax.ShapeDtypeStruct(sums.shape, F32),
        ),
        in_specs=[pl.BlockSpec(memory_space=pltpu.SMEM), vmem, vmem, vmem],
        out_specs=(vmem, vmem),
        scratch_shapes=[
            pltpu.VMEM((revs, own.shape[0] // 2) + own.shape[1:], BF16),
            pltpu.VMEM((revs, own.shape[0] // 2) + own.shape[1:], BF16),
            pltpu.VMEM((shards,) + own.shape, BF16),
            pltpu.VMEM((7,) + sums.shape, F32),
            pltpu.VMEM((shards,) + sums.shape, F32),
            pltpu.SemaphoreType.DMA((2, 3 * shards)),
            pltpu.SemaphoreType.DMA((2, 3 * shards)),
            pltpu.SemaphoreType.DMA((16,)),
            pltpu.SemaphoreType.DMA((16,)),
            pltpu.SemaphoreType.DMA((3,)),
            pltpu.SemaphoreType.DMA((3,)),
        ],
        compiler_params=pltpu.CompilerParams(
            collective_id=1, has_side_effects=True, vmem_limit_bytes=40 << 20
        ),
    )(partner, own, other, sums)
    return gathered.reshape((shards * own.shape[0],) + own.shape[1:]), summed


def split_rows(matrix):
    high = matrix.astype(BF16)
    low = (matrix - high.astype(F32)).astype(BF16)
    return jnp.concatenate([high, low], axis=0)


def block_matrix(blocks):
    count, m, n = blocks.shape
    if count == 1:
        return blocks[0]
    eye = jnp.eye(count, dtype=F32)
    return (blocks[:, :, None, :] * eye[:, None, :, None]).reshape(count * m, count * n)


def block_parts(matrix, count):
    rows, cols = matrix.shape
    split = matrix.reshape(count, rows // count, count, cols // count)
    return jnp.stack([split[b, :, b, :] for b in range(count)])


def local(fields, out_grads, partner, kept_blocks, weight_in, bias_in, weight_out):
    shards = lax.axis_size("row")
    channels, rows, n_cols = fields.shape[1:]
    n_rows = rows * shards
    count, bs = weight_out.shape[0], weight_out.shape[-1]
    own_rev = lax.axis_index("rev")
    row_rank = lax.axis_index("row")
    slots = KY // shards
    scale = 1.0 / math.sqrt(n_rows * n_cols)
    col_np = column_tables(n_cols)
    row_np = row_tables(n_rows, shards)
    col_table = jnp.asarray(col_np)
    row_table = lax.dynamic_index_in_dim(jnp.asarray(row_np), row_rank, 0, keepdims=False)
    inv_table = row_table.reshape(2, KY, rows).transpose(0, 2, 1).reshape(2 * rows, KY)

    revs = lax.axis_size("rev")
    part_f = forward_partial(fields[0], col_table, row_table, scale)
    target = partner[own_rev]

    def route(values):
        every = lax.all_gather(values, "rev", axis=0, tiled=False)
        return lax.dynamic_index_in_dim(every, target, 0, keepdims=False)

    own_kernels = revs == 8 and shards > 1
    if own_kernels:
        spectra, other, grad_spec = exchange(
            part_f, out_grads[0], col_table, row_table, partner, shards, revs, scale
        )
    else:
        part_g = forward_partial(out_grads[0], col_table, row_table, scale)
        spectra, grad_spec = (
            lax.psum_scatter(part, "row", scatter_dimension=0, tiled=True)
            for part in (part_f, part_g)
        )
        other = route(spectra)

    own_real = block_matrix(weight_in[:, 0, :bs])
    own_imag = block_matrix(weight_in[:, 1, :bs])
    other_real = block_matrix(weight_in[:, 0, bs:])
    other_imag = block_matrix(weight_in[:, 1, bs:])
    out_real = block_matrix(weight_out[:, 0])
    out_imag = block_matrix(weight_out[:, 1])
    win_t = jnp.concatenate(
        [
            jnp.concatenate([own_real, own_imag], axis=1),
            jnp.concatenate([-own_imag, own_real], axis=1),
            jnp.concatenate([other_real, other_imag], axis=1),
            jnp.concatenate([-other_imag, other_real], axis=1),
        ],
        axis=0,
    )
    wout_t = jnp.concatenate(
        [
            jnp.concatenate([out_real, out_imag], axis=1),
            jnp.concatenate([-out_imag, out_real], axis=1),
        ],
        axis=0,
    )
    bias = jnp.concatenate([bias_in[:, 0].reshape(-1), bias_in[:, 1].reshape(-1)])
    bias = jnp.broadcast_to(bias[:, None], (2 * channels, KX))
    own_grads, other_grads, sums = mlp(
        (row_rank * slots).reshape(1).astype(jnp.int32),
        kept_blocks[own_rev].reshape(1),
        spectra,
        other,
        grad_spec,
        split_rows(win_t.T),
        bias,
        split_rows(wout_t),
        split_rows(win_t),
    )
    if own_kernels:
        gathered, summed = finish(own_grads, other_grads, sums, partner, shards, revs)
    else:
        total = own_grads.astype(F32) + route(other_grads).astype(F32)
        gathered = lax.all_gather(total.astype(BF16), "row", axis=0, tiled=True)
        summed = lax.psum(sums, ("rev", "row"))
    field_grads = inverse_field(gathered, inv_table, col_table.T, scale)

    summed = summed * (1.0 / math.sqrt(revs * KX * KY))
    width = 2 * channels
    pre, cot = summed[:width], summed[width:]

    def complex_parts(grad):
        top, bottom = grad[:channels], grad[channels:]
        real = top[:, :channels] + bottom[:, channels:]
        imag = bottom[:, :channels] - top[:, channels:]
        return jnp.stack([block_parts(real.T, count), block_parts(imag.T, count)], axis=1)

    grad_win = jnp.concatenate(
        [complex_parts(pre[:, :width]), complex_parts(pre[:, width : 2 * width])], axis=2
    )
    grad_wout = complex_parts(cot[:, 2 * width : 3 * width])

    def bias_parts(column):
        return column.reshape(2, count, bs).transpose(1, 0, 2)

    return (
        field_grads[None],
        grad_win,
        bias_parts(pre[:, 3 * width]),
        grad_wout,
        bias_parts(cot[:, 3 * width]),
    )


def solution(mesh):
    placed = (P("rev", None, "row", None), P("rev", None, "row", None), P(), P(), P(), P(), P())
    return jax.shard_map(
        local,
        mesh=mesh,
        in_specs=placed,
        out_specs=(P("rev", None, "row", None), P(), P(), P(), P()),
        check_vma=False,
    )
```

```python
import functools
import math

import jax
import jax.numpy as jnp
import ml_dtypes
import numpy as np
from jax import lax
from jax.experimental import pallas as pl
from jax.experimental.pallas import tpu as pltpu
from jax.sharding import PartitionSpec as P

KX = 128
MB = 16
KY = 256
BF16 = jnp.bfloat16
F32 = jnp.float32
GELU_A = math.sqrt(2.0 / math.pi)
GELU_B = 0.044715


def column_tables(n_cols):
    phases = np.arange(n_cols)[:, None] * np.arange(KX)[None, :] % n_cols
    angles = phases.astype(np.float32) * np.float32(2.0 * math.pi / n_cols)
    both = np.concatenate([np.cos(angles), -np.sin(angles)], axis=1)
    return both.astype(ml_dtypes.bfloat16)


def row_tables(n_rows, shards):
    slot = np.arange(KY)
    signed = np.where(slot < KY // 2, slot, slot - KY + n_rows)
    phases = signed[:, None] * np.arange(n_rows)[None, :] % n_rows
    angles = phases.astype(np.float32) * np.float32(2.0 * math.pi / n_rows)
    both = np.concatenate([np.cos(angles), np.sin(angles)], axis=0)
    split = both.reshape(2 * KY, shards, n_rows // shards).transpose(1, 0, 2)
    return np.ascontiguousarray(split).astype(ml_dtypes.bfloat16)


def forward_channel(channels, scale, values, col_ref, row_ref, held, channel):
    cols = jnp.dot(values, col_ref[...], preferred_element_type=F32).astype(BF16)
    quads = jnp.dot(row_ref[...], cols, preferred_element_type=F32)
    real = (quads[:KY, :KX] + quads[KY:, KX:]) * scale
    imag = (quads[:KY, KX:] - quads[KY:, :KX]) * scale
    held[pl.ds(pl.multiple_of(channel * KY, KY), KY), :] = real
    held[pl.ds(pl.multiple_of((channels + channel) * KY, KY), KY), :] = imag


def forward_kernel(channels, group, scale, x_ref, col_ref, row_ref, out_ref, held):
    step = pl.program_id(0)
    for i in range(group):
        forward_channel(channels, scale, x_ref[i], col_ref, row_ref, held, step * group + i)

    @pl.when(step == channels // group - 1)
    def _():
        def turn(j, carry):
            out_ref[j] = held[pl.ds(j, 2 * channels, stride=KY), :].astype(BF16)
            return carry

        lax.fori_loop(0, KY, turn, 0, unroll=8)


def forward_partial(field, col_table, row_table, scale):
    channels, n_rows, n_cols = field.shape
    group = 4 if channels % 4 == 0 else 1
    return pl.pallas_call(
        functools.partial(forward_kernel, channels, group, scale),
        grid=(channels // group,),
        out_shape=jax.ShapeDtypeStruct((KY, 2 * channels, KX), BF16),
        in_specs=[
            pl.BlockSpec((group, n_rows, n_cols), lambda c: (c, 0, 0)),
            pl.BlockSpec((n_cols, 2 * KX), lambda c: (0, 0)),
            pl.BlockSpec((2 * KY, n_rows), lambda c: (0, 0)),
        ],
        out_specs=pl.BlockSpec((KY, 2 * channels, KX), lambda c: (0, 0, 0)),
        scratch_shapes=[pltpu.VMEM((2 * channels * KY, KX), F32)],
        compiler_params=pltpu.CompilerParams(
            dimension_semantics=("arbitrary",), vmem_limit_bytes=57 << 20
        ),
        cost_estimate=pl.CostEstimate(
            flops=channels * n_rows * 2 * KX * (2 * n_cols + 4 * KY),
            bytes_accessed=2 * field.size + 4 * KY * channels * KX,
            transcendentals=0,
        ),
    )(field, col_table, row_table)


def inverse_kernel(channels, scale, total_ref, row_ref, col_ref, out_ref, held):
    step = pl.program_id(0)

    @pl.when(step == 0)
    def _():
        def turn(j, carry):
            at = pl.multiple_of(j * 2 * channels, 2 * channels)
            held[pl.ds(at, 2 * channels), :] = total_ref[j].astype(F32)
            return carry

        lax.fori_loop(0, KY, turn, 0, unroll=8)

    for i in range(out_ref.shape[0]):
        channel = step * out_ref.shape[0] + i
        real = held[pl.ds(channel, KY, stride=2 * channels), :].astype(BF16)
        imag = held[pl.ds(channels + channel, KY, stride=2 * channels), :].astype(BF16)
        pair = jnp.concatenate([real, imag], axis=1)
        n_rows = out_ref.shape[1]
        quads = lax.dot_general(
            row_ref[...], pair, (((1,), (0,)), ((), ())), preferred_element_type=F32
        )
        rows_re = quads[:n_rows, :KX] - quads[n_rows:, KX:]
        rows_im = quads[n_rows:, :KX] + quads[:n_rows, KX:]
        rows = jnp.concatenate([rows_re, rows_im], axis=1).astype(BF16)
        field = jnp.dot(rows, col_ref[...], preferred_element_type=F32) * scale
        out_ref[i] = field.astype(BF16)


def inverse_field(total, row_table_t, col_table_t, scale):
    channels = total.shape[1] // 2
    n_rows, n_cols = row_table_t.shape[0] // 2, col_table_t.shape[1]
    group = 4 if channels % 4 == 0 else 1
    return pl.pallas_call(
        functools.partial(inverse_kernel, channels, scale),
        grid=(channels // group,),
        out_shape=jax.ShapeDtypeStruct((channels, n_rows, n_cols), BF16),
        in_specs=[
            pl.BlockSpec((KY, 2 * channels, KX), lambda c: (0, 0, 0)),
            pl.BlockSpec((2 * n_rows, KY), lambda c: (0, 0)),
            pl.BlockSpec((2 * KX, n_cols), lambda c: (0, 0)),
        ],
        out_specs=pl.BlockSpec((group, n_rows, n_cols), lambda c: (c, 0, 0)),
        scratch_shapes=[pltpu.VMEM((2 * channels * KY, KX), F32)],
        compiler_params=pltpu.CompilerParams(
            dimension_semantics=("arbitrary",), vmem_limit_bytes=32 << 20
        ),
        cost_estimate=pl.CostEstimate(
            flops=channels * n_rows * 2 * KX * (2 * n_cols + 4 * KY),
            bytes_accessed=2 * channels * n_rows * n_cols + 4 * KY * channels * KX,
            transcendentals=0,
        ),
    )(total, row_table_t, col_table_t)


def mlp_kernel(
    slots, group, width, slot0_ref, kept_ref, own_ref, other_ref, cot_ref, win_ref, bias_ref,
    wout_t_ref, win_t_ref, own_out, other_out, sums_ref,
):
    step = pl.program_id(0)

    @pl.when(step == 0)
    def _():
        sums_ref[...] = jnp.zeros_like(sums_ref)

    lanes = lax.broadcasted_iota(jnp.int32, (width, KX), 1)
    limit = kept_ref[0] * MB
    own, other, cot = [], [], []
    for g in range(group):
        slot = slot0_ref[0] + step * group + g
        extent = jnp.where(slot < KY // 2, slot, KY - slot)
        keep = jnp.maximum(lanes, extent) < limit
        own.append(own_ref[g])
        other.append(other_ref[g])
        cot.append(jnp.where(keep, cot_ref[g].astype(F32), 0.0).astype(BF16))
    joined = jnp.concatenate(
        [jnp.concatenate(own, axis=1), jnp.concatenate(other, axis=1)], axis=0
    )
    cotangent = jnp.concatenate(cot, axis=1)

    def times(weights, values):
        parts = jnp.dot(weights, values, preferred_element_type=F32)
        half = parts.shape[0] // 2
        return parts[:half] + parts[half:]

    pre = times(win_ref[...], joined) + bias_ref[:, 0:1]
    square = pre * pre
    bend = jnp.tanh(GELU_A * (pre + GELU_B * (square * pre)))
    hidden = 0.5 * pre * (1.0 + bend)
    slope = 0.5 * (1.0 + bend) + 0.5 * pre * (1.0 - bend * bend) * (
        GELU_A * (1.0 + (3.0 * GELU_B) * square)
    )
    grad_pre = (times(wout_t_ref[...], cotangent) * slope).astype(BF16)
    grad_joined = times(win_t_ref[...], grad_pre)
    for g in range(group):
        at = slice(g * KX, (g + 1) * KX)
        own_out[g] = grad_joined[:width, at].astype(BF16)
        other_out[g] = grad_joined[width:, at].astype(BF16)
    left = jnp.concatenate([grad_pre, cotangent], axis=0)
    ones = jnp.ones((width, group * KX), BF16)
    right = jnp.concatenate([joined, hidden.astype(BF16), ones], axis=0)
    sums_ref[...] += lax.dot_general(
        left, right, (((1,), (1,)), ((), ())), preferred_element_type=F32
    )


def mlp(slot0, kept, own, other, cot, win, bias, wout_t, win_t):
    slots, width, _ = own.shape
    group = 8
    while slots % group:
        group //= 2
    block = pl.BlockSpec((group, width, KX), lambda i: (i, 0, 0))
    scalar = pl.BlockSpec(memory_space=pltpu.SMEM)

    def whole(array):
        return pl.BlockSpec(array.shape, lambda i: (0, 0))

    return pl.pallas_call(
        functools.partial(mlp_kernel, slots, group, width),
        grid=(slots // group,),
        out_shape=(
            jax.ShapeDtypeStruct(own.shape, BF16),
            jax.ShapeDtypeStruct(own.shape, BF16),
            jax.ShapeDtypeStruct((2 * width, 4 * width), F32),
        ),
        in_specs=[
            scalar, scalar, block, block, block, whole(win), whole(bias), whole(wout_t), whole(win_t),
        ],
        out_specs=(block, block, pl.BlockSpec((2 * width, 4 * width), lambda i: (0, 0))),
        compiler_params=pltpu.CompilerParams(
            dimension_semantics=("arbitrary",), vmem_limit_bytes=32 << 20
        ),
        cost_estimate=pl.CostEstimate(
            flops=slots * KX * 2 * width * 16 * width,
            bytes_accessed=10 * own.size,
            transcendentals=slots * KX * width,
        ),
    )(slot0, kept, own, other, cot, win, bias, wout_t, win_t)


MESH = pl.DeviceIdType.MESH


class Line:
    def __init__(self, size, send_sems, recv_sems):
        self.size, self.send_sems, self.recv_sems = size, send_sems, recv_sems
        self.me = lax.axis_index("row")

    def copy(self, side, tag, source, target):
        return pltpu.make_async_remote_copy(
            src_ref=source,
            dst_ref=target,
            send_sem=self.send_sems.at[side, tag],
            recv_sem=self.recv_sems.at[side, tag],
            device_id={"row": self.me + 1 - 2 * side},
            device_id_type=MESH,
        )


class Cube:
    def __init__(self, slots, send_sems, recv_sems, base=0):
        self.slots, self.send_sems, self.recv_sems = slots, send_sems, recv_sems
        self.base = base
        self.me = lax.axis_index("rev")
        core, x, y = self.me % 2, (self.me // 2) % 2, self.me // 4
        self.step = {"c": 1 - 2 * core, "x": 2 - 4 * x, "y": 4 - 8 * y}

    def copy(self, tag, axis, slot, part=None):
        block = self.slots.at[slot]
        if part is not None:
            half = self.slots.shape[1] // 2
            block = self.slots.at[slot, pl.ds(part * half, half)]
        return pltpu.make_async_remote_copy(
            src_ref=block,
            dst_ref=block,
            send_sem=self.send_sems.at[self.base + tag],
            recv_sem=self.recv_sems.at[self.base + tag],
            device_id={"rev": self.me + self.step[axis]},
            device_id_type=MESH,
        )

    def numbered(self, tag):
        me, step = self.me, self.step
        axis, slot, part = (
            ("x", me, None),
            ("y", me, None),
            ("c", me, None),
            ("y", me + step["x"], 0),
            ("x", me + step["y"], 1),
            ("c", me + step["x"], None),
            ("c", me + step["y"], None),
            ("c", me + step["x"] + step["y"], None),
        )[tag]
        return self.copy(tag, axis, slot, part)

    def received(self, *tags):
        for tag in tags:
            self.numbered(tag).wait_recv()

    def start(self, *tags):
        for tag in tags:
            self.numbered(tag).start()

    def first(self):
        self.start(0, 1, 2)

    def second(self):
        self.received(0, 1)
        self.start(3, 4, 5, 6)

    def third(self):
        self.received(3, 4)
        self.start(7)

    def last(self):
        self.received(2, 5, 6, 7)
        for tag in range(8):
            self.numbered(tag).wait_send()


def greet(size, with_cube):
    me = lax.axis_index("row")
    barrier = pltpu.get_barrier_semaphore()
    sides = ((me < size - 1, me + 1), (me > 0, me - 1))
    for there, neighbour in sides:

        @pl.when(there)
        def _(neighbour=neighbour):
            pl.semaphore_signal(
                barrier, inc=1, device_id={"row": neighbour}, device_id_type=MESH
            )

    if with_cube:
        rev = lax.axis_index("rev")
        core, x, y = rev % 2, (rev // 2) % 2, rev // 4
        for other in (rev + 1 - 2 * core, rev + 2 - 4 * x, rev + 4 - 8 * y):
            pl.semaphore_signal(barrier, inc=1, device_id={"rev": other}, device_id_type=MESH)

    at_end = (me == 0) | (me == size - 1)
    around = 3 if with_cube else 0

    @pl.when(at_end)
    def _():
        pl.semaphore_wait(barrier, around + 1)

    @pl.when(jnp.logical_not(at_end))
    def _():
        pl.semaphore_wait(barrier, around + 2)


def add_into(held, side, slot, part_ref):
    held[side, slot] = (held[side, slot].astype(F32) + part_ref[slot].astype(F32)).astype(BF16)


def reduce_step(line, held, base, part_ref, t):
    n, me = line.size, line.me
    for side in (0, 1):
        place = me if side == 0 else n - 1 - me
        slot = n - 1 - t + me if side == 0 else t - (n - 1 - me)
        ahead = 1 if side == 0 else -1

        @pl.when((place <= t) & (place < n - 1))
        def _(side=side, place=place, slot=slot, ahead=ahead):
            copy = line.copy(side, base + slot, held.at[side, slot], held.at[side, slot])

            @pl.when(place > 0)
            def _():
                copy.wait_recv()
                add_into(held, side, slot, part_ref)

            @pl.when(place == 0)
            def _():
                held[side, slot] = part_ref[slot]

            @pl.when(place < t)
            def _():
                old = slot + ahead
                line.copy(side, base + old, held.at[side, old], held.at[side, old]).wait_send()

            copy.start()


def reduce_last(line, held, base, part_ref, out_ref):
    n, me = line.size, line.me
    for side in (0, 1):
        place = me if side == 0 else n - 1 - me
        ahead = 1 if side == 0 else -1

        @pl.when(place > 0)
        def _(side=side):
            line.copy(side, base + me, held.at[side, me], held.at[side, me]).wait_recv()

    @pl.when((me > 0) & (me < n - 1))
    def _():
        total = part_ref[me].astype(F32) + held[0, me].astype(F32) + held[1, me].astype(F32)
        out_ref[...] = total.astype(BF16)

    @pl.when(me == 0)
    def _():
        out_ref[...] = (part_ref[me].astype(F32) + held[1, me].astype(F32)).astype(BF16)

    @pl.when(me == n - 1)
    def _():
        out_ref[...] = (part_ref[me].astype(F32) + held[0, me].astype(F32)).astype(BF16)


def reduce_sent(line, held, base):
    n, me = line.size, line.me
    for side in (0, 1):
        place = me if side == 0 else n - 1 - me
        slot = me + 1 if side == 0 else me - 1

        @pl.when(place < n - 1)
        def _(side=side, slot=slot):
            line.copy(side, base + slot, held.at[side, slot], held.at[side, slot]).wait_send()


def exchange_kernel(
    n, channels, scale, partner_ref, part_f, field_ref, col_ref, row_ref, own_ref, other_ref,
    cot_ref, held_f, held_g, slots, field, spread, part_g, line_send, line_recv, cube_send,
    cube_recv, field_sem,
):
    fetch = pltpu.make_async_copy(field_ref, field, field_sem)
    fetch.start()
    greet(n, True)
    line = Line(n, line_send, line_recv)
    cube = Cube(slots, cube_send, cube_recv)

    def transform(channel, carry):
        forward_channel(channels, scale, field[channel], col_ref, row_ref, spread, channel)
        return carry

    for t in range(n - 1):
        reduce_step(line, held_f, 0, part_f, t)
        if t == 0:
            fetch.wait()
        lax.fori_loop(channels * t // (n - 1), channels * (t + 1) // (n - 1), transform, 0)
    rows = KY // n
    for shard in range(n):

        def turn(j, carry, shard=shard):
            values = spread[pl.ds(shard * rows + j, 2 * channels, stride=KY), :]
            part_g[shard, j] = values.astype(BF16)
            return carry

        lax.fori_loop(0, rows, turn, 0, unroll=8)
    reduce_last(line, held_f, 0, part_f, own_ref)
    slots[cube.me] = own_ref[...]
    reduce_sent(line, held_f, 0)
    cube.first()
    for t in range(n - 1):
        reduce_step(line, held_g, n, part_g, t)
        if t == 0:
            cube.second()
        if t == 1:
            cube.third()
    if n < 3:
        cube.third()
    reduce_last(line, held_g, n, part_g, cot_ref)
    reduce_sent(line, held_g, n)
    cube.last()
    other_ref[...] = slots[partner_ref[cube.me]]


def exchange(part_f, field_g, col_table, row_table, partner, shards, revs, scale):
    slots, width = part_f.shape[0] // shards, part_f.shape[1]
    block = (slots, width, KX)
    vmem = pl.BlockSpec(memory_space=pltpu.VMEM)
    shape = jax.ShapeDtypeStruct(block, BF16)
    return pl.pallas_call(
        functools.partial(exchange_kernel, shards, width // 2, scale),
        out_shape=(shape, shape, shape),
        in_specs=[
            pl.BlockSpec(memory_space=pltpu.SMEM), vmem, pl.BlockSpec(memory_space=pl.ANY), vmem, vmem,
        ],
        out_specs=(vmem, vmem, vmem),
        scratch_shapes=[
            pltpu.VMEM((2, shards) + block, BF16),
            pltpu.VMEM((2, shards) + block, BF16),
            pltpu.VMEM((revs,) + block, BF16),
            pltpu.VMEM(field_g.shape, BF16),
            pltpu.VMEM((width * KY, KX), F32),
            pltpu.VMEM((shards,) + block, BF16),
            pltpu.SemaphoreType.DMA((2, 2 * shards)),
            pltpu.SemaphoreType.DMA((2, 2 * shards)),
            pltpu.SemaphoreType.DMA((8,)),
            pltpu.SemaphoreType.DMA((8,)),
            pltpu.SemaphoreType.DMA,
        ],
        compiler_params=pltpu.CompilerParams(
            collective_id=0, has_side_effects=True, vmem_limit_bytes=44 << 20
        ),
    )(partner, part_f.reshape((shards,) + block), field_g, col_table, row_table)


def finish_kernel(
    n, revs, partner_ref, own_ref, other_ref, sums_ref, all_ref, total_ref, slots_a,
    slots_b, gathered, small, small_rows, line_send, line_recv, cube_send, cube_recv, small_send, small_recv,
):
    greet(n, True)
    line = Line(n, line_send, line_recv)
    half = own_ref.shape[0] // 2
    buffers = (slots_a, slots_b)
    cubes = [Cube(buffers[h], cube_send, cube_recv, 8 * h) for h in (0, 1)]
    rev, me = cubes[0].me, line.me
    for h in (0, 1):
        buffers[h][rev] = other_ref[h * half : (h + 1) * half]
    small[0] = sums_ref[...]

    def small_copy(i):
        return pltpu.make_async_remote_copy(
            src_ref=small.at[i],
            dst_ref=small.at[4 + i],
            send_sem=small_send.at[i],
            recv_sem=small_recv.at[i],
            device_id={"rev": rev + cubes[0].step["xyc"[i]]},
            device_id_type=MESH,
        )

    def small_add(i):
        small_copy(i).wait_recv()
        small[i + 1] = small[i] + small[4 + i]

    def add_half(h):
        part = pl.ds(h * half, half)
        other = buffers[h][partner_ref[rev]]
        gathered[me, part] = (own_ref[part].astype(F32) + other.astype(F32)).astype(BF16)

    def row_copies(side, slot, h):
        block = gathered.at[slot, pl.ds(h * half, half)]
        copies = [line.copy(side, h * n + slot, block, block)]
        if h == 0:
            few = small_rows.at[slot]
            copies.insert(0, line.copy(side, 2 * n + slot, few, few))
        return copies

    def row_step(t, h):
        for side in (0, 1):
            place = me if side == 0 else n - 1 - me
            slot = me - t if side == 0 else me + t
            old = me - t + 1 if side == 0 else me + t - 1
            if t > 0:

                @pl.when(place >= t)
                def _(side=side, slot=slot):
                    for copy in row_copies(side, slot, h):
                        copy.wait_recv()

                @pl.when((place >= t - 1) & (place < n - 1))
                def _(side=side, old=old):
                    for copy in row_copies(side, old, h):
                        copy.wait_send()

            if t < n - 1:

                @pl.when((place >= t) & (place < n - 1))
                def _(side=side, slot=slot):
                    for copy in row_copies(side, slot, h):
                        copy.start()

    small_copy(0).start()
    cubes[0].first()
    small_add(0)
    small_copy(1).start()
    cubes[0].second()
    cubes[1].first()
    small_add(1)
    small_copy(2).start()
    cubes[0].third()
    small_add(2)
    small_rows[me] = small[3]
    cubes[0].last()
    for i in range(3):
        small_copy(i).wait_send()
    add_half(0)
    row_step(0, 0)
    cubes[1].second()
    cubes[1].third()
    cubes[1].last()
    add_half(1)
    row_step(0, 1)
    for t in range(1, n):
        row_step(t, 0)
        row_step(t, 1)

    all_ref[...] = gathered[...]
    summed = small_rows[0]
    for i in range(1, n):
        summed = summed + small_rows[i]
    total_ref[...] = summed


def finish(own, other, sums, partner, shards, revs):
    vmem = pl.BlockSpec(memory_space=pltpu.VMEM)
    gathered, summed = pl.pallas_call(
        functools.partial(finish_kernel, shards, revs),
        out_shape=(
            jax.ShapeDtypeStruct((shards,) + own.shape, BF16),
            jax.ShapeDtypeStruct(sums.shape, F32),
        ),
        in_specs=[pl.BlockSpec(memory_space=pltpu.SMEM), vmem, vmem, vmem],
        out_specs=(vmem, vmem),
        scratch_shapes=[
            pltpu.VMEM((revs, own.shape[0] // 2) + own.shape[1:], BF16),
            pltpu.VMEM((revs, own.shape[0] // 2) + own.shape[1:], BF16),
            pltpu.VMEM((shards,) + own.shape, BF16),
            pltpu.VMEM((7,) + sums.shape, F32),
            pltpu.VMEM((shards,) + sums.shape, F32),
            pltpu.SemaphoreType.DMA((2, 3 * shards)),
            pltpu.SemaphoreType.DMA((2, 3 * shards)),
            pltpu.SemaphoreType.DMA((16,)),
            pltpu.SemaphoreType.DMA((16,)),
            pltpu.SemaphoreType.DMA((3,)),
            pltpu.SemaphoreType.DMA((3,)),
        ],
        compiler_params=pltpu.CompilerParams(
            collective_id=1, has_side_effects=True, vmem_limit_bytes=40 << 20
        ),
    )(partner, own, other, sums)
    return gathered.reshape((shards * own.shape[0],) + own.shape[1:]), summed


def split_rows(matrix):
    high = matrix.astype(BF16)
    low = (matrix - high.astype(F32)).astype(BF16)
    return jnp.concatenate([high, low], axis=0)


def block_matrix(blocks):
    count, m, n = blocks.shape
    if count == 1:
        return blocks[0]
    eye = jnp.eye(count, dtype=F32)
    return (blocks[:, :, None, :] * eye[:, None, :, None]).reshape(count * m, count * n)


def block_parts(matrix, count):
    rows, cols = matrix.shape
    split = matrix.reshape(count, rows // count, count, cols // count)
    return jnp.stack([split[b, :, b, :] for b in range(count)])


def local(fields, out_grads, partner, kept_blocks, weight_in, bias_in, weight_out):
    shards = lax.axis_size("row")
    channels, rows, n_cols = fields.shape[1:]
    n_rows = rows * shards
    count, bs = weight_out.shape[0], weight_out.shape[-1]
    own_rev = lax.axis_index("rev")
    row_rank = lax.axis_index("row")
    slots = KY // shards
    scale = 1.0 / math.sqrt(n_rows * n_cols)
    col_np = column_tables(n_cols)
    row_np = row_tables(n_rows, shards)
    col_table = jnp.asarray(col_np)
    row_table = lax.dynamic_index_in_dim(jnp.asarray(row_np), row_rank, 0, keepdims=False)
    inv_table = row_table.reshape(2, KY, rows).transpose(0, 2, 1).reshape(2 * rows, KY)

    revs = lax.axis_size("rev")
    part_f = forward_partial(fields[0], col_table, row_table, scale)
    target = partner[own_rev]

    def route(values):
        every = lax.all_gather(values, "rev", axis=0, tiled=False)
        return lax.dynamic_index_in_dim(every, target, 0, keepdims=False)

    own_kernels = revs == 8 and shards > 1
    if own_kernels:
        spectra, other, grad_spec = exchange(
            part_f, out_grads[0], col_table, row_table, partner, shards, revs, scale
        )
    else:
        part_g = forward_partial(out_grads[0], col_table, row_table, scale)
        spectra, grad_spec = (
            lax.psum_scatter(part, "row", scatter_dimension=0, tiled=True)
            for part in (part_f, part_g)
        )
        other = route(spectra)

    own_real = block_matrix(weight_in[:, 0, :bs])
    own_imag = block_matrix(weight_in[:, 1, :bs])
    other_real = block_matrix(weight_in[:, 0, bs:])
    other_imag = block_matrix(weight_in[:, 1, bs:])
    out_real = block_matrix(weight_out[:, 0])
    out_imag = block_matrix(weight_out[:, 1])
    win_t = jnp.concatenate(
        [
            jnp.concatenate([own_real, own_imag], axis=1),
            jnp.concatenate([-own_imag, own_real], axis=1),
            jnp.concatenate([other_real, other_imag], axis=1),
            jnp.concatenate([-other_imag, other_real], axis=1),
        ],
        axis=0,
    )
    wout_t = jnp.concatenate(
        [
            jnp.concatenate([out_real, out_imag], axis=1),
            jnp.concatenate([-out_imag, out_real], axis=1),
        ],
        axis=0,
    )
    bias = jnp.concatenate([bias_in[:, 0].reshape(-1), bias_in[:, 1].reshape(-1)])
    bias = jnp.broadcast_to(bias[:, None], (2 * channels, KX))
    own_grads, other_grads, sums = mlp(
        (row_rank * slots).reshape(1).astype(jnp.int32),
        kept_blocks[own_rev].reshape(1),
        spectra,
        other,
        grad_spec,
        split_rows(win_t.T),
        bias,
        split_rows(wout_t),
        split_rows(win_t),
    )
    if own_kernels:
        gathered, summed = finish(own_grads, other_grads, sums, partner, shards, revs)
    else:
        total = own_grads.astype(F32) + route(other_grads).astype(F32)
        gathered = lax.all_gather(total.astype(BF16), "row", axis=0, tiled=True)
        summed = lax.psum(sums, ("rev", "row"))
    field_grads = inverse_field(gathered, inv_table, col_table.T, scale)

    summed = summed * (1.0 / math.sqrt(revs * KX * KY))
    width = 2 * channels
    pre, cot = summed[:width], summed[width:]

    def complex_parts(grad):
        top, bottom = grad[:channels], grad[channels:]
        real = top[:, :channels] + bottom[:, channels:]
        imag = bottom[:, :channels] - top[:, channels:]
        return jnp.stack([block_parts(real.T, count), block_parts(imag.T, count)], axis=1)

    grad_win = jnp.concatenate(
        [complex_parts(pre[:, :width]), complex_parts(pre[:, width : 2 * width])], axis=2
    )
    grad_wout = complex_parts(cot[:, 2 * width : 3 * width])

    def bias_parts(column):
        return column.reshape(2, count, bs).transpose(1, 0, 2)

    return (
        field_grads[None],
        grad_win,
        bias_parts(pre[:, 3 * width]),
        grad_wout,
        bias_parts(cot[:, 3 * width]),
    )


def solution(mesh):
    placed = (P("rev", None, "row", None), P("rev", None, "row", None), P(), P(), P(), P(), P())
    return jax.shard_map(
        local,
        mesh=mesh,
        in_specs=placed,
        out_specs=(P("rev", None, "row", None), P(), P(), P(), P()),
        check_vma=False,
    )
```
